32 devices in a mesh: grp: 2 (over y), seq: 4 (over z), head: 2 (over x), sub: 2 (over core).
Axes of the slice: x: 2, y: 2, z: 4, core: 2. Of those that a mesh axis runs over, the one named last changes fastest.
Arguments:
- vid_q: bfloat16 [2560, 4096], P(('grp', 'seq', 'sub'), 'head'), parts along dimension 0, may hold values from -6 to 6
- vid_k: bfloat16 [2560, 4096], P(('grp', 'seq', 'sub'), 'head'), parts along dimension 0, may hold values from -6 to 6
- vid_v: bfloat16 [2560, 4096], P(('grp', 'seq', 'sub'), 'head'), parts along dimension 0, may hold values from -6 to 6
- aud_q: bfloat16 [640, 2048], P(('grp', 'seq', 'sub'), 'head'), parts along dimension 0, may hold values from -6 to 6
- cross_k: bfloat16 [2560, 2048], P(('grp', 'seq', 'sub'), 'head'), parts along dimension 0, may hold values from -6 to 6
- cross_v: bfloat16 [2560, 2048], P(('grp', 'seq', 'sub'), 'head'), parts along dimension 0, may hold values from -6 to 6
- cross_q: bfloat16 [2560, 2048], P(('grp', 'seq', 'sub'), 'head'), parts along dimension 0, may hold values from -6 to 6
- aud_k: bfloat16 [640, 2048], P(('grp', 'seq', 'sub'), 'head'), parts along dimension 0, may hold values from -6 to 6
- aud_v: bfloat16 [640, 2048], P(('grp', 'seq', 'sub'), 'head'), parts along dimension 0, may hold values from -6 to 6
- windows: int32 [2, 80], P(None, 'grp'), parts along dimension 1, may hold values from 0 to 40, as said below
Outputs:
- video_self: bfloat16 [2560, 4096], P(('grp', 'seq', 'sub'), 'head'), parts along dimension 0
- audio_out: bfloat16 [640, 2048], P(('grp', 'seq', 'sub'), 'head'), parts along dimension 0
- video_cross: bfloat16 [2560, 2048], P(('grp', 'seq', 'sub'), 'head'), parts along dimension 0
The draws below stay inside these ranges and needn't reach their ends.
There are 2 independent parts, one for each index of `grp`. The reference program is written for one: setup_inputs(seed, part) draws one part's arguments, and reference() takes and returns one part's arrays. A program takes and returns all parts, laid end to end along the dimension named above; each array names one. Nothing has to cross between parts.
Inputs may be any that keep to these rules, and one draw needn't show every extreme that they name: For every stretch c, windows[0, c] lies between max(0, c - 5) and c, and windows[1, c] between c + 1 and min(40, c + 6); in every draw some stretch reaches 5 tiles on both sides.
All inputs are finite; a program needn't handle non-finite values.
Results may differ from the reference program's by a relative error of at most 0.03.
Values may be sent and summed in bfloat16 or wider, within the bound.
A program may use at most 64 MiB of HBM per device.

```python
import jax
import jax.numpy as jnp
from jax import lax

VIDEO_HEADS = 32
HEAD_DIM = 128
AUDIO_HEADS = 32
AUDIO_DIM = 64
TILE_LEN = 32
STRETCH_LEN = 8
WINDOW_REACH = 5
VIDEO_TOKENS = 1280
AUDIO_TOKENS = 320
TILE_COUNT = 40


def drawn(key, query_rows, key_rows, width):
    base_query = jnp.clip(jax.random.normal(jax.random.fold_in(key, 11), (query_rows, width), jnp.float32), -5.0, 5.0)
    base_key = jnp.clip(jax.random.normal(jax.random.fold_in(key, 12), (key_rows, width), jnp.float32), -5.0, 5.0)
    return (base_query, base_key)


def video_pair(key):
    return drawn(jax.random.fold_in(key, 1), VIDEO_TOKENS, VIDEO_TOKENS, VIDEO_HEADS * HEAD_DIM)


def audio_pair(key):
    return drawn(jax.random.fold_in(key, 2), AUDIO_TOKENS, VIDEO_TOKENS, AUDIO_HEADS * AUDIO_DIM)


def window_pair(key):
    return drawn(jax.random.fold_in(key, 3), VIDEO_TOKENS, AUDIO_TOKENS, AUDIO_HEADS * AUDIO_DIM)


def draw_vid_q(key, part):
    return video_pair(key)[0].astype(jnp.bfloat16)


def draw_vid_k(key, part):
    return video_pair(key)[1].astype(jnp.bfloat16)


def draw_aud_q(key, part):
    return audio_pair(key)[0].astype(jnp.bfloat16)


def draw_cross_k(key, part):
    return audio_pair(key)[1].astype(jnp.bfloat16)


def draw_cross_q(key, part):
    return window_pair(key)[0].astype(jnp.bfloat16)


def draw_aud_k(key, part):
    return window_pair(key)[1].astype(jnp.bfloat16)


def draw_windows(key, part):
    below = jax.random.randint(jax.random.fold_in(key, 41), (TILE_COUNT,), 0, WINDOW_REACH + 1)
    above = jax.random.randint(jax.random.fold_in(key, 42), (TILE_COUNT,), 0, WINDOW_REACH + 1)
    chosen = jax.random.randint(jax.random.fold_in(key, 43), (), WINDOW_REACH, TILE_COUNT - WINDOW_REACH)
    below = below.at[chosen].set(WINDOW_REACH)
    above = above.at[chosen].set(WINDOW_REACH)
    stretch_ids = jnp.arange(TILE_COUNT, dtype=jnp.int32)
    first_tile = jnp.maximum(stretch_ids - below, 0)
    after_tile = jnp.minimum(stretch_ids + 1 + above, TILE_COUNT)
    return jnp.stack([first_tile, after_tile]).astype(jnp.int32)


def levels(stream_key, extent, cuts, low, largest):
    loudness, own = 1.0, jax.random.fold_in(stream_key, 6)
    for dim, parts in cuts:
        heights = jnp.exp(jax.random.uniform(jax.random.fold_in(own, dim), (parts,), jnp.float32, low / len(cuts), largest / len(cuts)))
        loudness = loudness * jnp.repeat(heights, extent[dim] // parts).reshape([-1 if axis == dim else 1 for axis in range(len(extent))])
    return loudness


def normal_values(own_key, shape, deviation, limit, cuts=(), held_as=jnp.bfloat16):
    values = jax.random.normal(own_key, shape, jnp.float32) * deviation
    if len(cuts) > 0:
        values = levels(own_key, shape, cuts, -0.22, 0.18) * values
    return jnp.clip(values, min=-limit, max=limit).astype(held_as)


def setup_inputs(seed: int = 0, part: int = 0) -> dict:
    key_of = jax.random.split(jax.random.key(seed), 11)
    part_keys = jax.random.split(jax.random.fold_in(key_of[10], part), 11)
    return {
        "vid_q": draw_vid_q(jax.random.fold_in(jax.random.fold_in(key_of[10], part), 71), part),
        "vid_k": draw_vid_k(jax.random.fold_in(jax.random.fold_in(key_of[10], part), 71), part),
        "vid_v": normal_values(part_keys[2], (VIDEO_TOKENS, VIDEO_HEADS * HEAD_DIM), 1.0, 6.0, ((0, 8), (1, 2))),
        "aud_q": draw_aud_q(jax.random.fold_in(jax.random.fold_in(key_of[10], part), 71), part),
        "cross_k": draw_cross_k(jax.random.fold_in(jax.random.fold_in(key_of[10], part), 71), part),
        "cross_v": normal_values(part_keys[5], (VIDEO_TOKENS, AUDIO_HEADS * AUDIO_DIM), 1.0, 6.0, ((0, 8), (1, 2))),
        "cross_q": draw_cross_q(jax.random.fold_in(jax.random.fold_in(key_of[10], part), 71), part),
        "aud_k": draw_aud_k(jax.random.fold_in(jax.random.fold_in(key_of[10], part), 71), part),
        "aud_v": normal_values(part_keys[8], (AUDIO_TOKENS, AUDIO_HEADS * AUDIO_DIM), 1.0, 6.0, ((0, 8), (1, 2))),
        "windows": draw_windows(jax.random.fold_in(jax.random.fold_in(key_of[10], part), 71), part),
    }


def attend(queries, key_rows, value_rows, scaling, visible):
    scores = jnp.dot(queries, key_rows.T, preferred_element_type=jnp.float32) * scaling
    scores = jnp.where(visible, scores, jnp.float32(-1e30))
    peak = jnp.max(scores, axis=1, keepdims=True)
    weights = jnp.exp(scores - peak)
    summed = jnp.sum(weights, axis=1, keepdims=True)
    mixed = jnp.dot(weights.astype(jnp.bfloat16), value_rows, preferred_element_type=jnp.float32)
    return mixed / summed


def split_heads(matrix, head_count):
    return matrix.reshape(matrix.shape[0], head_count, -1).transpose(1, 0, 2)


def multi_head(queries, key_rows, value_rows, head_count, head_size, visible):
    scaling = 1.0 / (head_size ** 0.5)

    def one_head(triple):
        return attend(triple[0], triple[1], triple[2], scaling, visible)

    stacked = lax.map(one_head, (split_heads(queries, head_count), split_heads(key_rows, head_count), split_heads(value_rows, head_count)))
    return stacked.transpose(1, 0, 2).reshape(queries.shape[0], -1).astype(jnp.bfloat16)


def reference(vid_q, vid_k, vid_v, aud_q, cross_k, cross_v, cross_q, aud_k, aud_v, windows):
    video_self = multi_head(vid_q, vid_k, vid_v, VIDEO_HEADS, HEAD_DIM, True)
    audio_out = multi_head(aud_q, cross_k, cross_v, AUDIO_HEADS, AUDIO_DIM, True)
    video_tile = jnp.arange(VIDEO_TOKENS, dtype=jnp.int32) // TILE_LEN
    audio_stretch = jnp.arange(AUDIO_TOKENS, dtype=jnp.int32) // STRETCH_LEN
    first_tile = windows[0][audio_stretch]
    after_tile = windows[1][audio_stretch]
    visible = (first_tile[None, :] <= video_tile[:, None]) & (video_tile[:, None] < after_tile[None, :])
    video_cross = multi_head(cross_q, aud_k, aud_v, AUDIO_HEADS, AUDIO_DIM, visible)
    return video_self, audio_out, video_cross
```

```python
from functools import partial
import math

import jax
import jax.numpy as jnp
from jax import lax
from jax.experimental import pallas as pl
from jax.experimental.pallas import tpu as pltpu
from jax.sharding import PartitionSpec as P

HEAD_DIM = 128
AUDIO_DIM = 64
TILE_LEN = 32
STRETCH_LEN = 8


def extended(cells, sides, width):
    for axis, dim in sides:
        count = lax.axis_size(axis)
        ends = count - 1
        head = lax.slice_in_dim(cells, 0, width, axis=dim)
        tail = lax.slice_in_dim(cells, cells.shape[dim] - width, cells.shape[dim], axis=dim)
        cells = jnp.concatenate(
            [
                lax.ppermute(tail, axis, [(i, (i + 1) % count) for i in range(ends)]),
                cells,
                lax.ppermute(head, axis, [((i + 1) % count, i) for i in range(ends)]),
            ],
            axis=dim,
        )
    return cells


def start_state(query_count, head_count, head_size):
    running = jnp.full((head_count, query_count), -jnp.inf, jnp.float32)
    summed = jnp.zeros((head_count, query_count), jnp.float32)
    numerator = jnp.zeros((head_count, query_count, head_size), jnp.float32)
    return (running, summed, numerator)


def absorb(state_in, queries, key_rows, value_rows, head_count, scaling, visible):
    running, summed, numerator = state_in
    query_count = queries.shape[0]
    key_count = key_rows.shape[0]
    head_size = queries.shape[1] // head_count
    scores = (
        jnp.einsum(
            "qhe,khe->hqk",
            queries.reshape(query_count, head_count, head_size),
            key_rows.reshape(key_count, head_count, head_size),
            preferred_element_type=jnp.float32,
        )
        * scaling
    )
    if visible is not None:
        scores = jnp.where(visible[None], scores, jnp.float32(-1e30))
    newest = jnp.maximum(running, jnp.max(scores, axis=2))
    shrink = jnp.exp(running - newest)
    weights = jnp.exp(scores - newest[:, :, None])
    summed = summed * shrink + jnp.sum(weights, axis=2)
    numerator = numerator * shrink[:, :, None] + jnp.einsum(
        "hqk,khe->hqe",
        weights.astype(jnp.bfloat16),
        value_rows.reshape(key_count, head_count, head_size),
        preferred_element_type=jnp.float32,
    )
    return (newest, summed, numerator)


def block_split(total_rows):
    block_rows = total_rows
    while block_rows > 512 and block_rows % 2 == 0:
        block_rows = block_rows // 2
    return (block_rows, total_rows // block_rows)


def fold_keys(state_in, shards_in, offset, queries, head_count, scaling):
    key_rows, value_rows = shards_in
    block_rows, block_count = block_split(key_rows.shape[0])
    key_blocks = key_rows.reshape(block_count, block_rows, key_rows.shape[1])
    value_blocks = value_rows.reshape(block_count, block_rows, value_rows.shape[1])

    def one_block(state, paired):
        return (absorb(state, queries, paired[0], paired[1], head_count, scaling, None), None)

    result, unused = lax.scan(one_block, state_in, (key_blocks, value_blocks))
    return result


def normalize_heads(state_in):
    running, summed, numerator = state_in
    mixed = numerator / summed[:, :, None]
    return mixed.transpose(1, 0, 2).reshape(mixed.shape[1], -1).astype(jnp.bfloat16)


def gathered_body(vid_q, vid_k, vid_v, aud_q, cross_k, cross_v, cross_q, aud_k, aud_v, windows):
    video_heads = vid_q.shape[1] // HEAD_DIM
    video_scaling = 1.0 / math.sqrt(HEAD_DIM)
    audio_heads = aud_q.shape[1] // AUDIO_DIM
    audio_scaling = 1.0 / math.sqrt(AUDIO_DIM)
    moved_q, moved_k, moved_v = (
        lax.all_to_all(vid_q, "sub", split_axis=1, concat_axis=0, tiled=True),
        lax.all_to_all(vid_k, "sub", split_axis=1, concat_axis=0, tiled=True),
        lax.all_to_all(vid_v, "sub", split_axis=1, concat_axis=0, tiled=True),
    )
    pair_heads = video_heads // lax.axis_size("sub")
    folder = partial(fold_keys, queries=moved_q, head_count=pair_heads, scaling=video_scaling)
    state = folder(
        start_state(moved_q.shape[0], pair_heads, HEAD_DIM),
        (
            lax.all_gather(moved_k, "seq", axis=0, tiled=True),
            lax.all_gather(moved_v, "seq", axis=0, tiled=True),
        ),
        jnp.int32(0),
    )
    video_self = lax.all_to_all(
        normalize_heads(state), "sub", split_axis=0, concat_axis=1, tiled=True
    )
    folder = partial(fold_keys, queries=aud_q, head_count=audio_heads, scaling=audio_scaling)
    state = folder(
        start_state(aud_q.shape[0], audio_heads, AUDIO_DIM),
        (
            lax.all_gather(cross_k, ("seq", "sub"), axis=0, tiled=True),
            lax.all_gather(cross_v, ("seq", "sub"), axis=0, tiled=True),
        ),
        jnp.int32(0),
    )
    audio_out = normalize_heads(state)
    audio_rows = aud_k.shape[0]
    key_width = aud_k.shape[1]
    padded_rows = extended(
        jnp.concatenate((aud_k, aud_v), axis=1), ((("seq", "sub"), 0),), audio_rows
    )
    near_keys = padded_rows[:, :key_width]
    near_values = padded_rows[:, key_width:]
    position = lax.axis_index(("seq", "sub"))
    audio_index = (position - 1) * audio_rows + jnp.arange(padded_rows.shape[0], dtype=jnp.int32)
    stretch_index = audio_index // STRETCH_LEN
    stretch_ids = jnp.arange(windows.shape[1], dtype=jnp.int32)
    onehot = stretch_index[:, None] == stretch_ids[None, :]
    first_tile = jnp.sum(jnp.where(onehot, windows[0][None, :], 0), axis=1)
    after_tile = jnp.sum(jnp.where(onehot, windows[1][None, :], 0), axis=1)
    video_rows = cross_q.shape[0]
    video_tile = (position * video_rows + jnp.arange(video_rows, dtype=jnp.int32)) // TILE_LEN
    visible = (first_tile[None, :] <= video_tile[:, None]) & (
        video_tile[:, None] < after_tile[None, :]
    )
    state = absorb(
        start_state(video_rows, audio_heads, AUDIO_DIM),
        cross_q,
        near_keys,
        near_values,
        audio_heads,
        audio_scaling,
        visible,
    )
    video_cross = normalize_heads(state)
    return (video_self, audio_out, video_cross)


LANES = 128
AXES = ("seq", "sub")


def softmax_mix(queries, key_rows, value_rows, scaling, visible=None):
    scores = lax.dot_general(
        queries, key_rows, (((1,), (1,)), ((), ())), preferred_element_type=jnp.float32
    )
    if visible is not None:
        scores = jnp.where(visible, scores, jnp.float32(-1e30))
    peak = jnp.max(scores, axis=1, keepdims=True)
    weights = jnp.exp2((scores - peak) * jnp.float32(scaling * math.log2(math.e)))
    summed = jnp.sum(weights, axis=1, keepdims=True)
    mixed = jnp.dot(
        weights.astype(jnp.bfloat16), value_rows, preferred_element_type=jnp.float32
    )
    return mixed / summed


def lane_heads(block):
    wide = block.astype(jnp.float32)
    lane = lax.broadcasted_iota(jnp.int32, wide.shape, 1) // AUDIO_DIM
    parts = [jnp.where(lane == i, wide, 0.0) for i in range(LANES // AUDIO_DIM)]
    return jnp.concatenate(parts, axis=0).astype(jnp.bfloat16)


def merge_lane_heads(stacked, rows):
    lane = lax.broadcasted_iota(jnp.int32, (rows, LANES), 1) // AUDIO_DIM
    merged = stacked[:rows]
    for i in range(1, LANES // AUDIO_DIM):
        merged = jnp.where(lane == i, stacked[i * rows : (i + 1) * rows], merged)
    return merged


def exchange_kernel(
    count,
    sub_count,
    vid_q,
    vid_k,
    vid_v,
    aud_q,
    cross_k,
    cross_v,
    cross_q,
    aud_k,
    aud_v,
    windows,
    video_self,
    audio_out,
    video_cross,
    land_q,
    land_k,
    land_v,
    land_aq,
    land_ck,
    land_cv,
    mixed_v,
    mixed_a,
    near_k,
    near_v,
    local_cq,
    mixed_c,
    send_sem,
    recv_sem,
    near_send,
    near_recv,
    local_sem,
):
    rows = vid_q.shape[0]
    audio_rows = aud_q.shape[0]
    video_each = vid_q.shape[1] // HEAD_DIM // count
    blocks_each = aud_q.shape[1] // LANES // count
    video_scaling = 1.0 / math.sqrt(HEAD_DIM)
    audio_scaling = 1.0 / math.sqrt(AUDIO_DIM)
    me = lax.axis_index("seq") * sub_count + lax.axis_index("sub")

    def device(peer):
        return {"seq": peer // sub_count, "sub": peer % sub_count}

    def peer_at(t):
        half = (t + 1) // 2
        return (me + count // 2 + (1 - 2 * (t % 2)) * half) % count

    barrier = pltpu.get_barrier_semaphore()

    def greet(t, carry):
        pl.semaphore_signal(
            barrier, inc=1, device_id=device(peer_at(t)), device_id_type=pl.DeviceIdType.MESH
        )
        return carry

    lax.fori_loop(0, count - 1, greet, 0)

    own = [
        pltpu.make_async_copy(cross_q, local_cq, local_sem.at[0]),
        pltpu.make_async_copy(aud_k, near_k.at[1], local_sem.at[1]),
        pltpu.make_async_copy(aud_v, near_v.at[1], local_sem.at[2]),
    ]
    for copy in own:
        copy.start()

    def column(index):
        return pl.ds(pl.multiple_of(index * LANES, LANES), LANES)

    def row(index):
        return pl.ds(pl.multiple_of(index * rows, rows), rows)

    streams = []
    for h in range(video_each):
        for array, land in ((vid_k, land_k), (vid_v, land_v), (vid_q, land_q)):
            streams.append(
                (
                    lambda peer, array=array, h=h: array.at[:, column(peer * video_each + h)],
                    lambda source, land=land, h=h: land.at[h, row(source), :],
                )
            )
    for b in range(blocks_each):
        for array, land in ((cross_k, land_ck), (cross_v, land_cv)):
            streams.append(
                (
                    lambda peer, array=array, b=b: array.at[:, column(peer * blocks_each + b)],
                    lambda source, land=land, b=b: land.at[b, row(source), :],
                )
            )
        streams.append(
            (
                lambda peer, b=b: aud_q.at[:, column(peer * blocks_each + b)],
                lambda source, b=b: land_aq.at[b, source],
            )
        )
    results = []
    for h in range(video_each):
        results.append(
            (
                lambda peer, h=h: mixed_v.at[h, row(peer), :],
                lambda source, h=h: video_self.at[:, column(source * video_each + h)],
            )
        )
    for b in range(blocks_each):
        results.append(
            (
                lambda peer, b=b: mixed_a.at[b, peer],
                lambda source, b=b: audio_out.at[:, column(source * blocks_each + b)],
            )
        )
    ways = streams + results

    def outgoing(k, peer):
        return pltpu.make_async_remote_copy(
            src_ref=ways[k][0](peer),
            dst_ref=ways[k][1](me),
            send_sem=send_sem.at[k, peer],
            recv_sem=recv_sem.at[k, me],
            device_id=device(peer),
            device_id_type=pl.DeviceIdType.MESH,
        )

    def incoming(k, peer):
        return pltpu.make_async_remote_copy(
            src_ref=ways[k][0](peer),
            dst_ref=ways[k][1](peer),
            send_sem=send_sem.at[k, peer],
            recv_sem=recv_sem.at[k, peer],
            device_id=device(peer),
            device_id_type=pl.DeviceIdType.MESH,
        )

    def kept(k):
        return pltpu.make_async_copy(ways[k][0](me), ways[k][1](me), send_sem.at[k, me])

    def near_copy(j, array, near, side, peer):
        return pltpu.make_async_remote_copy(
            src_ref=array,
            dst_ref=near.at[side],
            send_sem=near_send.at[j],
            recv_sem=near_recv.at[j],
            device_id=device(peer),
            device_id_type=pl.DeviceIdType.MESH,
        )

    for k in range(len(streams)):
        kept(k).start()
    pl.semaphore_wait(barrier, count - 1)

    near_pairs = ((0, aud_k, near_k), (1, aud_v, near_v))

    @pl.when(me < count - 1)
    def _():
        for j, array, near in near_pairs:
            near_copy(j, array, near, 0, me + 1).start()

    @pl.when(me > 0)
    def _():
        for j, array, near in near_pairs:
            near_copy(2 + j, array, near, 2, me - 1).start()

    for k in range(len(streams)):

        def send(t, carry, k=k):
            outgoing(k, peer_at(t)).start()
            return carry

        lax.fori_loop(0, count - 1, send, 0)

    @pl.when(me == 0)
    def _():
        for j, array, near in near_pairs:
            near[0] = jnp.zeros(near.shape[1:], near.dtype)

    @pl.when(me == count - 1)
    def _():
        for j, array, near in near_pairs:
            near[2] = jnp.zeros(near.shape[1:], near.dtype)

    for copy in own:
        copy.wait()

    @pl.when(me > 0)
    def _():
        for j, array, near in near_pairs:
            near_copy(j, array, near, 0, me - 1).wait_recv()

    @pl.when(me < count - 1)
    def _():
        for j, array, near in near_pairs:
            near_copy(2 + j, array, near, 2, me + 1).wait_recv()

    spans = windows.shape[1]
    tile = (me * rows + lax.broadcasted_iota(jnp.int32, (rows, spans), 0)) // TILE_LEN
    bounds = windows[...]
    inside = (bounds[0:1, :] <= tile) & (tile < bounds[1:2, :])
    inside = jnp.where(inside, 1.0, 0.0).astype(jnp.bfloat16)
    seen = []
    for side in range(3):
        stretch = lax.broadcasted_iota(jnp.int32, (spans, audio_rows), 1) // STRETCH_LEN
        stretch = stretch + (me + side - 1) * (audio_rows // STRETCH_LEN)
        picks = stretch == lax.broadcasted_iota(jnp.int32, (spans, audio_rows), 0)
        picks = jnp.where(picks, 1.0, 0.0).astype(jnp.bfloat16)
        part = jnp.dot(inside, picks, preferred_element_type=jnp.float32)
        seen.append(jnp.concatenate([part] * (LANES // AUDIO_DIM), axis=0))

    for b in range(cross_q.shape[1] // LANES):
        lanes = slice(b * LANES, (b + 1) * LANES)
        stacked = lane_heads(local_cq[:, lanes])
        scores = []
        for side in range(3):
            part = lax.dot_general(
                stacked,
                near_k[side, :, lanes],
                (((1,), (1,)), ((), ())),
                preferred_element_type=jnp.float32,
            )
            scores.append(jnp.where(seen[side] > 0.5, part, jnp.float32(-1e30)))
        peak = jnp.max(jnp.maximum(jnp.maximum(scores[0], scores[1]), scores[2]), axis=1, keepdims=True)
        factor = jnp.float32(audio_scaling * math.log2(math.e))
        weights = [jnp.exp2((part - peak) * factor) for part in scores]
        summed = jnp.sum(weights[0] + weights[1] + weights[2], axis=1, keepdims=True)
        mixed = sum(
            jnp.dot(
                weights[side].astype(jnp.bfloat16),
                near_v[side, :, lanes],
                preferred_element_type=jnp.float32,
            )
            for side in range(3)
        )
        mixed_c[:, lanes] = merge_lane_heads(mixed / summed, rows).astype(jnp.bfloat16)

    def await_stream(k):
        kept(k).wait()

        def one(t, carry):
            incoming(k, peer_at(t)).wait_recv()
            return carry

        lax.fori_loop(0, count - 1, one, 0)

    def run_blocks(k, mix):
        def one(t, carry):
            mix(peer_at(t))

            @pl.when(t > 0)
            def _():
                outgoing(k, peer_at(t - 1)).start()

            return carry

        lax.fori_loop(0, count, one, 0)

    first = len(streams)
    for h in range(video_each):
        for k in range(3 * h, 3 * h + 3):
            await_stream(k)

        def mix_video(source, h=h):
            mixed = softmax_mix(land_q[h, row(source), :], land_k[h], land_v[h], video_scaling)
            mixed_v[h, row(source), :] = mixed.astype(jnp.bfloat16)

        run_blocks(first + h, mix_video)
        if h == 0:
            finished = pltpu.make_async_copy(mixed_c, video_cross, local_sem.at[0])
            finished.start()
    for b in range(blocks_each):
        base = 3 * video_each + 3 * b
        for k in range(base, base + 3):
            await_stream(k)

        def mix_audio(source, b=b):
            mixed = softmax_mix(
                lane_heads(land_aq[b, source]), land_ck[b], land_cv[b], audio_scaling
            )
            mixed_a[b, source] = merge_lane_heads(mixed, audio_rows).astype(jnp.bfloat16)

        run_blocks(first + video_each + b, mix_audio)
    for k in range(first, len(ways)):
        kept(k).start()

    for k in range(len(ways)):

        def sent(t, carry, k=k):
            outgoing(k, peer_at(t)).wait_send()
            return carry

        lax.fori_loop(0, count - 1, sent, 0)
    for k in range(first, len(ways)):
        await_stream(k)
    finished.wait()

    @pl.when(me < count - 1)
    def _():
        for j, array, near in near_pairs:
            near_copy(j, array, near, 0, me + 1).wait_send()

    @pl.when(me > 0)
    def _():
        for j, array, near in near_pairs:
            near_copy(2 + j, array, near, 2, me - 1).wait_send()


def exchanged_body(count, sub_count, *arrays):
    vid_q, vid_k, vid_v, aud_q, cross_k, cross_v, cross_q, aud_k, aud_v, windows = arrays
    rows = vid_q.shape[0]
    audio_rows = aud_q.shape[0]
    video_each = vid_q.shape[1] // HEAD_DIM // count
    blocks_each = aud_q.shape[1] // LANES // count
    kinds = 4 * video_each + 4 * blocks_each
    half = jnp.bfloat16
    place = pl.BlockSpec(memory_space=pl.ANY)
    return pl.pallas_call(
        partial(exchange_kernel, count, sub_count),
        out_shape=(
            jax.ShapeDtypeStruct(vid_q.shape, half),
            jax.ShapeDtypeStruct(aud_q.shape, half),
            jax.ShapeDtypeStruct(cross_q.shape, half),
        ),
        in_specs=[place] * 9 + [pl.BlockSpec(memory_space=pltpu.VMEM)],
        out_specs=(place, place, place),
        scratch_shapes=[
            pltpu.VMEM((video_each, count * rows, HEAD_DIM), half),
            pltpu.VMEM((video_each, count * rows, HEAD_DIM), half),
            pltpu.VMEM((video_each, count * rows, HEAD_DIM), half),
            pltpu.VMEM((blocks_each, count, audio_rows, LANES), half),
            pltpu.VMEM((blocks_each, count * rows, LANES), half),
            pltpu.VMEM((blocks_each, count * rows, LANES), half),
            pltpu.VMEM((video_each, count * rows, HEAD_DIM), half),
            pltpu.VMEM((blocks_each, count, audio_rows, LANES), half),
            pltpu.VMEM((3, audio_rows, aud_k.shape[1]), half),
            pltpu.VMEM((3, audio_rows, aud_k.shape[1]), half),
            pltpu.VMEM(cross_q.shape, half),
            pltpu.VMEM(cross_q.shape, half),
            pltpu.SemaphoreType.DMA((kinds, count)),
            pltpu.SemaphoreType.DMA((kinds, count)),
            pltpu.SemaphoreType.DMA((4,)),
            pltpu.SemaphoreType.DMA((4,)),
            pltpu.SemaphoreType.DMA((3,)),
        ],
        compiler_params=pltpu.CompilerParams(collective_id=0, has_side_effects=True),
        name="joint_attention",
    )(*arrays)


def body(*arrays):
    sub_count = lax.axis_size("sub")
    count = lax.axis_size("seq") * sub_count
    video_heads = arrays[0].shape[1] // HEAD_DIM
    audio_blocks = arrays[3].shape[1] // LANES
    if video_heads % count == 0 and audio_blocks % count == 0:
        return exchanged_body(count, sub_count, *arrays)
    return gathered_body(*arrays)


def solution(mesh):
    return jax.shard_map(
        body,
        mesh=mesh,
        in_specs=(
            P(("grp", "seq", "sub"), "head"),
            P(("grp", "seq", "sub"), "head"),
            P(("grp", "seq", "sub"), "head"),
            P(("grp", "seq", "sub"), "head"),
            P(("grp", "seq", "sub"), "head"),
            P(("grp", "seq", "sub"), "head"),
            P(("grp", "seq", "sub"), "head"),
            P(("grp", "seq", "sub"), "head"),
            P(("grp", "seq", "sub"), "head"),
            P(None, "grp"),
        ),
        out_specs=(
            P(("grp", "seq", "sub"), "head"),
            P(("grp", "seq", "sub"), "head"),
            P(("grp", "seq", "sub"), "head"),
        ),
        check_vma=False,
    )
```

```python
from functools import partial
import math

import jax
import jax.numpy as jnp
from jax import lax
from jax.experimental import pallas as pl
from jax.experimental.pallas import tpu as pltpu
from jax.sharding import PartitionSpec as P

HEAD_DIM = 128
AUDIO_DIM = 64
TILE_LEN = 32
STRETCH_LEN = 8


def extended(cells, sides, width):
    for axis, dim in sides:
        count = lax.axis_size(axis)
        ends = count - 1
        head = lax.slice_in_dim(cells, 0, width, axis=dim)
        tail = lax.slice_in_dim(cells, cells.shape[dim] - width, cells.shape[dim], axis=dim)
        cells = jnp.concatenate(
            [
                lax.ppermute(tail, axis, [(i, (i + 1) % count) for i in range(ends)]),
                cells,
                lax.ppermute(head, axis, [((i + 1) % count, i) for i in range(ends)]),
            ],
            axis=dim,
        )
    return cells


def start_state(query_count, head_count, head_size):
    running = jnp.full((head_count, query_count), -jnp.inf, jnp.float32)
    summed = jnp.zeros((head_count, query_count), jnp.float32)
    numerator = jnp.zeros((head_count, query_count, head_size), jnp.float32)
    return (running, summed, numerator)


def absorb(state_in, queries, key_rows, value_rows, head_count, scaling, visible):
    running, summed, numerator = state_in
    query_count = queries.shape[0]
    key_count = key_rows.shape[0]
    head_size = queries.shape[1] // head_count
    scores = (
        jnp.einsum(
            "qhe,khe->hqk",
            queries.reshape(query_count, head_count, head_size),
            key_rows.reshape(key_count, head_count, head_size),
            preferred_element_type=jnp.float32,
        )
        * scaling
    )
    if visible is not None:
        scores = jnp.where(visible[None], scores, jnp.float32(-1e30))
    newest = jnp.maximum(running, jnp.max(scores, axis=2))
    shrink = jnp.exp(running - newest)
    weights = jnp.exp(scores - newest[:, :, None])
    summed = summed * shrink + jnp.sum(weights, axis=2)
    numerator = numerator * shrink[:, :, None] + jnp.einsum(
        "hqk,khe->hqe",
        weights.astype(jnp.bfloat16),
        value_rows.reshape(key_count, head_count, head_size),
        preferred_element_type=jnp.float32,
    )
    return (newest, summed, numerator)


def block_split(total_rows):
    block_rows = total_rows
    while block_rows > 512 and block_rows % 2 == 0:
        block_rows = block_rows // 2
    return (block_rows, total_rows // block_rows)


def fold_keys(state_in, shards_in, offset, queries, head_count, scaling):
    key_rows, value_rows = shards_in
    block_rows, block_count = block_split(key_rows.shape[0])
    key_blocks = key_rows.reshape(block_count, block_rows, key_rows.shape[1])
    value_blocks = value_rows.reshape(block_count, block_rows, value_rows.shape[1])

    def one_block(state, paired):
        return (absorb(state, queries, paired[0], paired[1], head_count, scaling, None), None)

    result, unused = lax.scan(one_block, state_in, (key_blocks, value_blocks))
    return result


def normalize_heads(state_in):
    running, summed, numerator = state_in
    mixed = numerator / summed[:, :, None]
    return mixed.transpose(1, 0, 2).reshape(mixed.shape[1], -1).astype(jnp.bfloat16)


def gathered_body(vid_q, vid_k, vid_v, aud_q, cross_k, cross_v, cross_q, aud_k, aud_v, windows):
    video_heads = vid_q.shape[1] // HEAD_DIM
    video_scaling = 1.0 / math.sqrt(HEAD_DIM)
    audio_heads = aud_q.shape[1] // AUDIO_DIM
    audio_scaling = 1.0 / math.sqrt(AUDIO_DIM)
    moved_q, moved_k, moved_v = (
        lax.all_to_all(vid_q, "sub", split_axis=1, concat_axis=0, tiled=True),
        lax.all_to_all(vid_k, "sub", split_axis=1, concat_axis=0, tiled=True),
        lax.all_to_all(vid_v, "sub", split_axis=1, concat_axis=0, tiled=True),
    )
    pair_heads = video_heads // lax.axis_size("sub")
    folder = partial(fold_keys, queries=moved_q, head_count=pair_heads, scaling=video_scaling)
    state = folder(
        start_state(moved_q.shape[0], pair_heads, HEAD_DIM),
        (
            lax.all_gather(moved_k, "seq", axis=0, tiled=True),
            lax.all_gather(moved_v, "seq", axis=0, tiled=True),
        ),
        jnp.int32(0),
    )
    video_self = lax.all_to_all(
        normalize_heads(state), "sub", split_axis=0, concat_axis=1, tiled=True
    )
    folder = partial(fold_keys, queries=aud_q, head_count=audio_heads, scaling=audio_scaling)
    state = folder(
        start_state(aud_q.shape[0], audio_heads, AUDIO_DIM),
        (
            lax.all_gather(cross_k, ("seq", "sub"), axis=0, tiled=True),
            lax.all_gather(cross_v, ("seq", "sub"), axis=0, tiled=True),
        ),
        jnp.int32(0),
    )
    audio_out = normalize_heads(state)
    audio_rows = aud_k.shape[0]
    key_width = aud_k.shape[1]
    padded_rows = extended(
        jnp.concatenate((aud_k, aud_v), axis=1), ((("seq", "sub"), 0),), audio_rows
    )
    near_keys = padded_rows[:, :key_width]
    near_values = padded_rows[:, key_width:]
    position = lax.axis_index(("seq", "sub"))
    audio_index = (position - 1) * audio_rows + jnp.arange(padded_rows.shape[0], dtype=jnp.int32)
    stretch_index = audio_index // STRETCH_LEN
    stretch_ids = jnp.arange(windows.shape[1], dtype=jnp.int32)
    onehot = stretch_index[:, None] == stretch_ids[None, :]
    first_tile = jnp.sum(jnp.where(onehot, windows[0][None, :], 0), axis=1)
    after_tile = jnp.sum(jnp.where(onehot, windows[1][None, :], 0), axis=1)
    video_rows = cross_q.shape[0]
    video_tile = (position * video_rows + jnp.arange(video_rows, dtype=jnp.int32)) // TILE_LEN
    visible = (first_tile[None, :] <= video_tile[:, None]) & (
        video_tile[:, None] < after_tile[None, :]
    )
    state = absorb(
        start_state(video_rows, audio_heads, AUDIO_DIM),
        cross_q,
        near_keys,
        near_values,
        audio_heads,
        audio_scaling,
        visible,
    )
    video_cross = normalize_heads(state)
    return (video_self, audio_out, video_cross)


LANES = 128
AXES = ("seq", "sub")


def softmax_mix(queries, key_rows, value_rows, scaling):
    scores = lax.dot_general(
        queries, key_rows, (((1,), (1,)), ((), ())), preferred_element_type=jnp.float32
    )
    peak = jnp.max(scores, axis=1, keepdims=True)
    weights = jnp.exp2((scores - peak) * jnp.float32(scaling * math.log2(math.e)))
    summed = jnp.sum(weights, axis=1, keepdims=True)
    mixed = jnp.dot(
        weights.astype(jnp.bfloat16), value_rows, preferred_element_type=jnp.float32
    )
    return mixed / summed, peak, summed


def lane_heads(block):
    wide = block.astype(jnp.float32)
    lane = lax.broadcasted_iota(jnp.int32, wide.shape, 1) // AUDIO_DIM
    parts = [jnp.where(lane == i, wide, 0.0) for i in range(LANES // AUDIO_DIM)]
    return jnp.concatenate(parts, axis=0).astype(jnp.bfloat16)


def merge_lane_heads(stacked, rows):
    lane = lax.broadcasted_iota(jnp.int32, (rows, LANES), 1) // AUDIO_DIM
    merged = stacked[:rows]
    for i in range(1, LANES // AUDIO_DIM):
        merged = jnp.where(lane == i, stacked[i * rows : (i + 1) * rows], merged)
    return merged


def exchange_kernel(
    count,
    sub_count,
    vid_q,
    vid_k,
    vid_v,
    aud_q,
    cross_k,
    cross_v,
    cross_q,
    aud_k,
    aud_v,
    windows,
    video_self,
    audio_out,
    video_cross,
    land_q,
    land_k,
    land_v,
    land_aq,
    land_ck,
    land_cv,
    mixed_v,
    mixed_a,
    own_part,
    own_stat,
    far_part,
    far_stat,
    got_part,
    got_stat,
    near_k,
    near_v,
    local_cq,
    mixed_c,
    send_sem,
    recv_sem,
    near_send,
    near_recv,
    part_send,
    part_recv,
    local_sem,
):
    rows = vid_q.shape[0]
    audio_rows = aud_q.shape[0]
    video_each = vid_q.shape[1] // HEAD_DIM // count
    half = count // 2
    blocks_each = aud_q.shape[1] // LANES // half
    width = blocks_each * LANES
    video_scaling = 1.0 / math.sqrt(HEAD_DIM)
    audio_scaling = 1.0 / math.sqrt(AUDIO_DIM)
    me = lax.axis_index("seq") * sub_count + lax.axis_index("sub")

    side = me // half
    place = me % half

    def device(peer):
        return {"seq": peer // sub_count, "sub": peer % sub_count}

    def peer_at(t):
        return (me + half + (1 - 2 * (t % 2)) * ((t + 1) // 2)) % count

    def peer_near(t):
        return side * half + (place + 1 + t) % half

    barrier = pltpu.get_barrier_semaphore()

    def greet(t, carry):
        pl.semaphore_signal(
            barrier, inc=1, device_id=device(peer_at(t)), device_id_type=pl.DeviceIdType.MESH
        )
        return carry

    lax.fori_loop(0, count - 1, greet, 0)

    own = [
        pltpu.make_async_copy(cross_q, local_cq, local_sem.at[0]),
        pltpu.make_async_copy(aud_k, near_k.at[1], local_sem.at[1]),
        pltpu.make_async_copy(aud_v, near_v.at[1], local_sem.at[2]),
    ]
    for copy in own:
        copy.start()

    def column(index):
        return pl.ds(pl.multiple_of(index * LANES, LANES), LANES)

    def row(index):
        return pl.ds(pl.multiple_of(index * rows, rows), rows)

    def columns(index):
        return pl.ds(pl.multiple_of(index * width, LANES), width)

    def video_way(array, land, h):
        return (
            lambda peer: array.at[:, column(peer * video_each + h)],
            lambda source: land.at[h, row(source), :],
            peer_at,
            count - 1,
        )

    def half_way(array, land):
        return (
            lambda peer: array.at[:, columns(peer % half)],
            lambda source: land.at[row(source % half), :],
            peer_near,
            half - 1,
        )

    ways = [
        (
            lambda peer: aud_q.at[:, columns(peer % half)],
            lambda source: land_aq.at[source],
            peer_at,
            count - 1,
        )
    ]
    audio_ways = [0]
    video_ways = []
    for h in range(video_each):
        video_ways.append(list(range(len(ways), len(ways) + 3)))
        for array, land in ((vid_k, land_k), (vid_v, land_v), (vid_q, land_q)):
            ways.append(video_way(array, land, h))
        if h == 0:
            for array, land in ((cross_k, land_ck), (cross_v, land_cv)):
                audio_ways.append(len(ways))
                ways.append(half_way(array, land))
    first = len(ways)
    for h in range(video_each):
        ways.append(
            (
                lambda peer, h=h: mixed_v.at[h, row(peer), :],
                lambda source, h=h: video_self.at[:, column(source * video_each + h)],
                peer_at,
                count - 1,
            )
        )
    ways.append(
        (
            lambda peer: mixed_a.at[peer % half],
            lambda source: audio_out.at[:, columns(source % half)],
            peer_near,
            half - 1,
        )
    )

    def outgoing(k, peer):
        return pltpu.make_async_remote_copy(
            src_ref=ways[k][0](peer),
            dst_ref=ways[k][1](me),
            send_sem=send_sem.at[k, peer],
            recv_sem=recv_sem.at[k, me],
            device_id=device(peer),
            device_id_type=pl.DeviceIdType.MESH,
        )

    def incoming(k, peer):
        return pltpu.make_async_remote_copy(
            src_ref=ways[k][0](peer),
            dst_ref=ways[k][1](peer),
            send_sem=send_sem.at[k, peer],
            recv_sem=recv_sem.at[k, peer],
            device_id=device(peer),
            device_id_type=pl.DeviceIdType.MESH,
        )

    def kept(k):
        return pltpu.make_async_copy(ways[k][0](me), ways[k][1](me), send_sem.at[k, me])

    def near_copy(j, array, near, side, peer):
        return pltpu.make_async_remote_copy(
            src_ref=array,
            dst_ref=near.at[side],
            send_sem=near_send.at[j],
            recv_sem=near_recv.at[j],
            device_id=device(peer),
            device_id_type=pl.DeviceIdType.MESH,
        )

    for k in range(first):
        kept(k).start()
    pl.semaphore_wait(barrier, count - 1)

    near_pairs = ((0, aud_k, near_k), (1, aud_v, near_v))

    @pl.when(me < count - 1)
    def _():
        for j, array, near in near_pairs:
            near_copy(j, array, near, 0, me + 1).start()

    @pl.when(me > 0)
    def _():
        for j, array, near in near_pairs:
            near_copy(2 + j, array, near, 2, me - 1).start()

    for k in range(first):

        def send(t, carry, k=k):
            outgoing(k, ways[k][2](t)).start()
            return carry

        lax.fori_loop(0, ways[k][3], send, 0)

    @pl.when(me == 0)
    def _():
        for j, array, near in near_pairs:
            near[0] = jnp.zeros(near.shape[1:], near.dtype)

    @pl.when(me == count - 1)
    def _():
        for j, array, near in near_pairs:
            near[2] = jnp.zeros(near.shape[1:], near.dtype)

    for copy in own:
        copy.wait()

    @pl.when(me > 0)
    def _():
        for j, array, near in near_pairs:
            near_copy(j, array, near, 0, me - 1).wait_recv()

    @pl.when(me < count - 1)
    def _():
        for j, array, near in near_pairs:
            near_copy(2 + j, array, near, 2, me + 1).wait_recv()

    spans = windows.shape[1]
    tile = (me * rows + lax.broadcasted_iota(jnp.int32, (rows, spans), 0)) // TILE_LEN
    bounds = windows[...]
    inside = (bounds[0:1, :] <= tile) & (tile < bounds[1:2, :])
    inside = jnp.where(inside, 1.0, 0.0).astype(jnp.bfloat16)
    seen = []
    for slot in range(3):
        stretch = lax.broadcasted_iota(jnp.int32, (spans, audio_rows), 1) // STRETCH_LEN
        stretch = stretch + (me + slot - 1) * (audio_rows // STRETCH_LEN)
        picks = stretch == lax.broadcasted_iota(jnp.int32, (spans, audio_rows), 0)
        picks = jnp.where(picks, 1.0, 0.0).astype(jnp.bfloat16)
        part = jnp.dot(inside, picks, preferred_element_type=jnp.float32)
        seen.append(jnp.concatenate([part] * (LANES // AUDIO_DIM), axis=0))

    for b in range(cross_q.shape[1] // LANES):
        lanes = slice(b * LANES, (b + 1) * LANES)
        stacked = lane_heads(local_cq[:, lanes])
        scores = []
        for slot in range(3):
            part = lax.dot_general(
                stacked,
                near_k[slot, :, lanes],
                (((1,), (1,)), ((), ())),
                preferred_element_type=jnp.float32,
            )
            scores.append(jnp.where(seen[slot] > 0.5, part, jnp.float32(-1e30)))
        peak = jnp.max(jnp.maximum(jnp.maximum(scores[0], scores[1]), scores[2]), axis=1, keepdims=True)
        factor = jnp.float32(audio_scaling * math.log2(math.e))
        weights = [jnp.exp2((part - peak) * factor) for part in scores]
        summed = jnp.sum(weights[0] + weights[1] + weights[2], axis=1, keepdims=True)
        mixed = sum(
            jnp.dot(
                weights[slot].astype(jnp.bfloat16),
                near_v[slot, :, lanes],
                preferred_element_type=jnp.float32,
            )
            for slot in range(3)
        )
        mixed_c[:, lanes] = merge_lane_heads(mixed / summed, rows).astype(jnp.bfloat16)

    def await_stream(k):
        kept(k).wait()

        def one(t, carry):
            incoming(k, ways[k][2](t)).wait_recv()
            return carry

        lax.fori_loop(0, ways[k][3], one, 0)

    def run_blocks(k, steps, mix):
        def one(t, carry):
            mix(ways[k][2](t))

            @pl.when(t > 0)
            def _():
                outgoing(k, ways[k][2](t - 1)).start()

            return carry

        lax.fori_loop(0, steps, one, 0)
        kept(k).start()

    def part_copy(j, array, land):
        return pltpu.make_async_remote_copy(
            src_ref=array,
            dst_ref=land,
            send_sem=part_send.at[j],
            recv_sem=part_recv.at[j],
            device_id=device((me + half) % count),
            device_id_type=pl.DeviceIdType.MESH,
        )

    part_copies = [part_copy(0, far_part, got_part), part_copy(1, far_stat, got_stat)]
    stat_lane = lax.broadcasted_iota(jnp.int32, (audio_rows, LANES), 1)
    each = LANES // AUDIO_DIM

    def audio_parts(first_source, part, stat):
        def one(j, stats):
            queries = land_aq[first_source + j]
            for b in range(blocks_each):
                lanes = slice(b * LANES, (b + 1) * LANES)
                mixed, peak, summed = softmax_mix(
                    lane_heads(queries[:, lanes]), land_ck[:, lanes], land_cv[:, lanes], audio_scaling
                )
                part[j, :, lanes] = merge_lane_heads(mixed, audio_rows).astype(part.dtype)
                level = peak * jnp.float32(audio_scaling * math.log2(math.e)) + jnp.log2(summed)
                for i in range(each):
                    stats = jnp.where(
                        stat_lane == (j * blocks_each + b) * each + i,
                        level[i * audio_rows : (i + 1) * audio_rows],
                        stats,
                    )
            return stats

        stat[...] = lax.fori_loop(0, half, one, jnp.zeros((audio_rows, LANES), jnp.float32))

    def merge_parts(peer):
        j = peer % half
        for b in range(blocks_each):
            lanes = slice(b * LANES, (b + 1) * LANES)
            shares = []
            for i in range(each):
                picked = stat_lane == (j * blocks_each + b) * each + i
                mine = jnp.sum(jnp.where(picked, own_stat[...], 0.0), axis=1, keepdims=True)
                other = jnp.sum(jnp.where(picked, got_stat[...], 0.0), axis=1, keepdims=True)
                peak = jnp.maximum(mine, other)
                mine = jnp.exp2(mine - peak)
                other = jnp.exp2(other - peak)
                total = mine + other
                shares.append((mine / total, other / total))
            own_share, got_share = (
                merge_lane_heads(
                    jnp.concatenate(
                        [jnp.broadcast_to(s[w], (audio_rows, LANES)) for s in shares], axis=0
                    ),
                    audio_rows,
                )
                for w in range(2)
            )
            merged = own_part[j, :, lanes] * own_share
            merged = merged + got_part[j, :, lanes].astype(jnp.float32) * got_share
            mixed_a[j, :, lanes] = merged.astype(jnp.bfloat16)

    for h in range(video_each):
        for k in video_ways[h]:
            await_stream(k)

        def mix_video(source, h=h):
            mixed, peak, summed = softmax_mix(
                land_q[h, row(source), :], land_k[h], land_v[h], video_scaling
            )
            mixed_v[h, row(source), :] = mixed.astype(jnp.bfloat16)

        run_blocks(first + h, count, mix_video)
        if h == 0:
            finished = pltpu.make_async_copy(mixed_c, video_cross, local_sem.at[0])
            finished.start()
            for k in audio_ways:
                await_stream(k)
            audio_parts((1 - side) * half, far_part, far_stat)
            audio_parts(side * half, own_part, own_stat)
            for copy in part_copies:
                copy.start()
    for copy in part_copies:
        copy.wait()
    run_blocks(len(ways) - 1, half, merge_parts)

    for k in range(len(ways)):

        def sent(t, carry, k=k):
            outgoing(k, ways[k][2](t)).wait_send()
            return carry

        lax.fori_loop(0, ways[k][3], sent, 0)
    for k in range(first, len(ways)):
        await_stream(k)
    finished.wait()

    @pl.when(me < count - 1)
    def _():
        for j, array, near in near_pairs:
            near_copy(j, array, near, 0, me + 1).wait_send()

    @pl.when(me > 0)
    def _():
        for j, array, near in near_pairs:
            near_copy(2 + j, array, near, 2, me - 1).wait_send()


def exchanged_body(count, sub_count, *arrays):
    vid_q, vid_k, vid_v, aud_q, cross_k, cross_v, cross_q, aud_k, aud_v, windows = arrays
    rows = vid_q.shape[0]
    audio_rows = aud_q.shape[0]
    video_each = vid_q.shape[1] // HEAD_DIM // count
    halves = count // 2
    width = aud_q.shape[1] // halves
    kinds = 4 * video_each + 4
    half = jnp.bfloat16
    place = pl.BlockSpec(memory_space=pl.ANY)
    return pl.pallas_call(
        partial(exchange_kernel, count, sub_count),
        out_shape=(
            jax.ShapeDtypeStruct(vid_q.shape, half),
            jax.ShapeDtypeStruct(aud_q.shape, half),
            jax.ShapeDtypeStruct(cross_q.shape, half),
        ),
        in_specs=[place] * 9 + [pl.BlockSpec(memory_space=pltpu.VMEM)],
        out_specs=(place, place, place),
        scratch_shapes=[
            pltpu.VMEM((video_each, count * rows, HEAD_DIM), half),
            pltpu.VMEM((video_each, count * rows, HEAD_DIM), half),
            pltpu.VMEM((video_each, count * rows, HEAD_DIM), half),
            pltpu.VMEM((count, audio_rows, width), half),
            pltpu.VMEM((halves * rows, width), half),
            pltpu.VMEM((halves * rows, width), half),
            pltpu.VMEM((video_each, count * rows, HEAD_DIM), half),
            pltpu.VMEM((halves, audio_rows, width), half),
            pltpu.VMEM((halves, audio_rows, width), jnp.float32),
            pltpu.VMEM((audio_rows, LANES), jnp.float32),
            pltpu.VMEM((halves, audio_rows, width), half),
            pltpu.VMEM((audio_rows, LANES), jnp.float32),
            pltpu.VMEM((halves, audio_rows, width), half),
            pltpu.VMEM((audio_rows, LANES), jnp.float32),
            pltpu.VMEM((3, audio_rows, aud_k.shape[1]), half),
            pltpu.VMEM((3, audio_rows, aud_k.shape[1]), half),
            pltpu.VMEM(cross_q.shape, half),
            pltpu.VMEM(cross_q.shape, half),
            pltpu.SemaphoreType.DMA((kinds, count)),
            pltpu.SemaphoreType.DMA((kinds, count)),
            pltpu.SemaphoreType.DMA((4,)),
            pltpu.SemaphoreType.DMA((4,)),
            pltpu.SemaphoreType.DMA((2,)),
            pltpu.SemaphoreType.DMA((2,)),
            pltpu.SemaphoreType.DMA((3,)),
        ],
        compiler_params=pltpu.CompilerParams(collective_id=0, has_side_effects=True),
        name="joint_attention",
    )(*arrays)


def body(*arrays):
    sub_count = lax.axis_size("sub")
    count = lax.axis_size("seq") * sub_count
    video_heads = arrays[0].shape[1] // HEAD_DIM
    audio_heads = arrays[3].shape[1] // AUDIO_DIM
    halved = lax.axis_size("seq") % 2 == 0 and audio_heads <= LANES
    if halved and video_heads % count == 0 and audio_heads % count == 0:
        return exchanged_body(count, sub_count, *arrays)
    return gathered_body(*arrays)


def solution(mesh):
    return jax.shard_map(
        body,
        mesh=mesh,
        in_specs=(
            P(("grp", "seq", "sub"), "head"),
            P(("grp", "seq", "sub"), "head"),
            P(("grp", "seq", "sub"), "head"),
            P(("grp", "seq", "sub"), "head"),
            P(("grp", "seq", "sub"), "head"),
            P(("grp", "seq", "sub"), "head"),
            P(("grp", "seq", "sub"), "head"),
            P(("grp", "seq", "sub"), "head"),
            P(("grp", "seq", "sub"), "head"),
            P(None, "grp"),
        ),
        out_specs=(
            P(("grp", "seq", "sub"), "head"),
            P(("grp", "seq", "sub"), "head"),
            P(("grp", "seq", "sub"), "head"),
        ),
        check_vma=False,
    )
```

```python
from functools import partial
import math

import jax
import jax.numpy as jnp
from jax import lax
from jax.experimental import pallas as pl
from jax.experimental.pallas import tpu as pltpu
from jax.sharding import PartitionSpec as P

HEAD_DIM = 128
AUDIO_DIM = 64
TILE_LEN = 32
STRETCH_LEN = 8


def extended(cells, sides, width):
    for axis, dim in sides:
        count = lax.axis_size(axis)
        ends = count - 1
        head = lax.slice_in_dim(cells, 0, width, axis=dim)
        tail = lax.slice_in_dim(cells, cells.shape[dim] - width, cells.shape[dim], axis=dim)
        cells = jnp.concatenate(
            [
                lax.ppermute(tail, axis, [(i, (i + 1) % count) for i in range(ends)]),
                cells,
                lax.ppermute(head, axis, [((i + 1) % count, i) for i in range(ends)]),
            ],
            axis=dim,
        )
    return cells


def start_state(query_count, head_count, head_size):
    running = jnp.full((head_count, query_count), -jnp.inf, jnp.float32)
    summed = jnp.zeros((head_count, query_count), jnp.float32)
    numerator = jnp.zeros((head_count, query_count, head_size), jnp.float32)
    return (running, summed, numerator)


def absorb(state_in, queries, key_rows, value_rows, head_count, scaling, visible):
    running, summed, numerator = state_in
    query_count = queries.shape[0]
    key_count = key_rows.shape[0]
    head_size = queries.shape[1] // head_count
    scores = (
        jnp.einsum(
            "qhe,khe->hqk",
            queries.reshape(query_count, head_count, head_size),
            key_rows.reshape(key_count, head_count, head_size),
            preferred_element_type=jnp.float32,
        )
        * scaling
    )
    if visible is not None:
        scores = jnp.where(visible[None], scores, jnp.float32(-1e30))
    newest = jnp.maximum(running, jnp.max(scores, axis=2))
    shrink = jnp.exp(running - newest)
    weights = jnp.exp(scores - newest[:, :, None])
    summed = summed * shrink + jnp.sum(weights, axis=2)
    numerator = numerator * shrink[:, :, None] + jnp.einsum(
        "hqk,khe->hqe",
        weights.astype(jnp.bfloat16),
        value_rows.reshape(key_count, head_count, head_size),
        preferred_element_type=jnp.float32,
    )
    return (newest, summed, numerator)


def block_split(total_rows):
    block_rows = total_rows
    while block_rows > 512 and block_rows % 2 == 0:
        block_rows = block_rows // 2
    return (block_rows, total_rows // block_rows)


def fold_keys(state_in, shards_in, offset, queries, head_count, scaling):
    key_rows, value_rows = shards_in
    block_rows, block_count = block_split(key_rows.shape[0])
    key_blocks = key_rows.reshape(block_count, block_rows, key_rows.shape[1])
    value_blocks = value_rows.reshape(block_count, block_rows, value_rows.shape[1])

    def one_block(state, paired):
        return (absorb(state, queries, paired[0], paired[1], head_count, scaling, None), None)

    result, unused = lax.scan(one_block, state_in, (key_blocks, value_blocks))
    return result


def normalize_heads(state_in):
    running, summed, numerator = state_in
    mixed = numerator / summed[:, :, None]
    return mixed.transpose(1, 0, 2).reshape(mixed.shape[1], -1).astype(jnp.bfloat16)


def gathered_body(vid_q, vid_k, vid_v, aud_q, cross_k, cross_v, cross_q, aud_k, aud_v, windows):
    video_heads = vid_q.shape[1] // HEAD_DIM
    video_scaling = 1.0 / math.sqrt(HEAD_DIM)
    audio_heads = aud_q.shape[1] // AUDIO_DIM
    audio_scaling = 1.0 / math.sqrt(AUDIO_DIM)
    moved_q, moved_k, moved_v = (
        lax.all_to_all(vid_q, "sub", split_axis=1, concat_axis=0, tiled=True),
        lax.all_to_all(vid_k, "sub", split_axis=1, concat_axis=0, tiled=True),
        lax.all_to_all(vid_v, "sub", split_axis=1, concat_axis=0, tiled=True),
    )
    pair_heads = video_heads // lax.axis_size("sub")
    folder = partial(fold_keys, queries=moved_q, head_count=pair_heads, scaling=video_scaling)
    state = folder(
        start_state(moved_q.shape[0], pair_heads, HEAD_DIM),
        (
            lax.all_gather(moved_k, "seq", axis=0, tiled=True),
            lax.all_gather(moved_v, "seq", axis=0, tiled=True),
        ),
        jnp.int32(0),
    )
    video_self = lax.all_to_all(
        normalize_heads(state), "sub", split_axis=0, concat_axis=1, tiled=True
    )
    folder = partial(fold_keys, queries=aud_q, head_count=audio_heads, scaling=audio_scaling)
    state = folder(
        start_state(aud_q.shape[0], audio_heads, AUDIO_DIM),
        (
            lax.all_gather(cross_k, ("seq", "sub"), axis=0, tiled=True),
            lax.all_gather(cross_v, ("seq", "sub"), axis=0, tiled=True),
        ),
        jnp.int32(0),
    )
    audio_out = normalize_heads(state)
    audio_rows = aud_k.shape[0]
    key_width = aud_k.shape[1]
    padded_rows = extended(
        jnp.concatenate((aud_k, aud_v), axis=1), ((("seq", "sub"), 0),), audio_rows
    )
    near_keys = padded_rows[:, :key_width]
    near_values = padded_rows[:, key_width:]
    position = lax.axis_index(("seq", "sub"))
    audio_index = (position - 1) * audio_rows + jnp.arange(padded_rows.shape[0], dtype=jnp.int32)
    stretch_index = audio_index // STRETCH_LEN
    stretch_ids = jnp.arange(windows.shape[1], dtype=jnp.int32)
    onehot = stretch_index[:, None] == stretch_ids[None, :]
    first_tile = jnp.sum(jnp.where(onehot, windows[0][None, :], 0), axis=1)
    after_tile = jnp.sum(jnp.where(onehot, windows[1][None, :], 0), axis=1)
    video_rows = cross_q.shape[0]
    video_tile = (position * video_rows + jnp.arange(video_rows, dtype=jnp.int32)) // TILE_LEN
    visible = (first_tile[None, :] <= video_tile[:, None]) & (
        video_tile[:, None] < after_tile[None, :]
    )
    state = absorb(
        start_state(video_rows, audio_heads, AUDIO_DIM),
        cross_q,
        near_keys,
        near_values,
        audio_heads,
        audio_scaling,
        visible,
    )
    video_cross = normalize_heads(state)
    return (video_self, audio_out, video_cross)


LANES = 128
AXES = ("seq", "sub")


def softmax_mix(queries, key_rows, value_rows, scaling):
    scores = lax.dot_general(
        queries, key_rows, (((1,), (1,)), ((), ())), preferred_element_type=jnp.float32
    )
    peak = jnp.max(scores, axis=1, keepdims=True)
    weights = jnp.exp2((scores - peak) * jnp.float32(scaling * math.log2(math.e)))
    summed = jnp.sum(weights, axis=1, keepdims=True)
    mixed = jnp.dot(
        weights.astype(jnp.bfloat16), value_rows, preferred_element_type=jnp.float32
    )
    return mixed / summed, peak, summed


def lane_heads(block):
    wide = block.astype(jnp.float32)
    lane = lax.broadcasted_iota(jnp.int32, wide.shape, 1) // AUDIO_DIM
    parts = [jnp.where(lane == i, wide, 0.0) for i in range(LANES // AUDIO_DIM)]
    return jnp.concatenate(parts, axis=0).astype(jnp.bfloat16)


def merge_lane_heads(stacked, rows):
    lane = lax.broadcasted_iota(jnp.int32, (rows, LANES), 1) // AUDIO_DIM
    merged = stacked[:rows]
    for i in range(1, LANES // AUDIO_DIM):
        merged = jnp.where(lane == i, stacked[i * rows : (i + 1) * rows], merged)
    return merged


def exchange_kernel(
    count,
    sub_count,
    vid_q,
    vid_k,
    vid_v,
    aud_q,
    cross_k,
    cross_v,
    cross_q,
    aud_k,
    aud_v,
    windows,
    video_self,
    audio_out,
    video_cross,
    land_q,
    land_k,
    land_v,
    land_aq,
    land_ck,
    land_cv,
    mixed_v,
    mixed_a,
    own_part,
    own_stat,
    far_part,
    far_stat,
    got_part,
    got_stat,
    near_k,
    near_v,
    local_cq,
    send_sem,
    recv_sem,
    near_send,
    near_recv,
    part_send,
    part_recv,
    local_sem,
):
    rows = vid_q.shape[0]
    audio_rows = aud_q.shape[0]
    video_each = vid_q.shape[1] // HEAD_DIM // count
    half = count // 2
    blocks_each = aud_q.shape[1] // LANES // half
    width = blocks_each * LANES
    video_scaling = 1.0 / math.sqrt(HEAD_DIM)
    audio_scaling = 1.0 / math.sqrt(AUDIO_DIM)
    me = lax.axis_index("seq") * sub_count + lax.axis_index("sub")

    side = me // half
    place = me % half

    def device(peer):
        return {"seq": peer // sub_count, "sub": peer % sub_count}

    def peer_at(t):
        return ((side + 1 - t // half) % 2) * half + (place + t + t // half) % half

    def peer_near(t):
        return side * half + (place + 1 + t) % half

    barrier = pltpu.get_barrier_semaphore()

    def greet(t, carry):
        pl.semaphore_signal(
            barrier, inc=1, device_id=device(peer_at(t)), device_id_type=pl.DeviceIdType.MESH
        )
        return carry

    lax.fori_loop(0, count - 1, greet, 0)

    own = [
        pltpu.make_async_copy(cross_q, local_cq, local_sem.at[0]),
        pltpu.make_async_copy(aud_k, near_k.at[1], local_sem.at[1]),
        pltpu.make_async_copy(aud_v, near_v.at[1], local_sem.at[2]),
    ]
    for copy in own:
        copy.start()

    def column(index):
        return pl.ds(pl.multiple_of(index * LANES, LANES), LANES)

    def row(index):
        return pl.ds(pl.multiple_of(index * rows, rows), rows)

    def columns(index):
        return pl.ds(pl.multiple_of(index * width, LANES), width)

    def video_way(array, land, h):
        return (
            lambda peer: array.at[:, column(peer * video_each + h)],
            lambda source: land.at[h, row(source), :],
            peer_at,
            count - 1,
        )

    def half_way(array, land):
        return (
            lambda peer: array.at[:, columns(peer % half)],
            lambda source: land.at[row(source % half), :],
            peer_near,
            half - 1,
        )

    ways = [
        (
            lambda peer: aud_q.at[:, columns(peer % half)],
            lambda source: land_aq.at[source],
            peer_at,
            count - 1,
        )
    ]
    audio_ways = [0]
    video_ways = []
    for h in range(video_each):
        video_ways.append(list(range(len(ways), len(ways) + 3)))
        for array, land in ((vid_k, land_k), (vid_v, land_v), (vid_q, land_q)):
            ways.append(video_way(array, land, h))
        if h == 0:
            for array, land in ((cross_k, land_ck), (cross_v, land_cv)):
                audio_ways.append(len(ways))
                ways.append(half_way(array, land))
    first = len(ways)
    for h in range(video_each):
        ways.append(
            (
                lambda peer, h=h: mixed_v.at[h, row(peer), :],
                lambda source, h=h: video_self.at[:, column(source * video_each + h)],
                peer_at,
                count - 1,
            )
        )
    ways.append(
        (
            lambda peer: mixed_a.at[peer % half],
            lambda source: audio_out.at[:, columns(source % half)],
            peer_near,
            half - 1,
        )
    )

    def outgoing(k, peer):
        return pltpu.make_async_remote_copy(
            src_ref=ways[k][0](peer),
            dst_ref=ways[k][1](me),
            send_sem=send_sem.at[k, peer],
            recv_sem=recv_sem.at[k, me],
            device_id=device(peer),
            device_id_type=pl.DeviceIdType.MESH,
        )

    def incoming(k, peer):
        return pltpu.make_async_remote_copy(
            src_ref=ways[k][0](peer),
            dst_ref=ways[k][1](peer),
            send_sem=send_sem.at[k, peer],
            recv_sem=recv_sem.at[k, peer],
            device_id=device(peer),
            device_id_type=pl.DeviceIdType.MESH,
        )

    def kept(k):
        return pltpu.make_async_copy(ways[k][0](me), ways[k][1](me), send_sem.at[k, me])

    def near_copy(j, array, near, side, peer):
        return pltpu.make_async_remote_copy(
            src_ref=array,
            dst_ref=near.at[side],
            send_sem=near_send.at[j],
            recv_sem=near_recv.at[j],
            device_id=device(peer),
            device_id_type=pl.DeviceIdType.MESH,
        )

    for k in range(first):
        kept(k).start()
    pl.semaphore_wait(barrier, count - 1)

    near_pairs = ((0, aud_k, near_k), (1, aud_v, near_v))

    @pl.when(me < count - 1)
    def _():
        for j, array, near in near_pairs:
            near_copy(j, array, near, 0, me + 1).start()

    @pl.when(me > 0)
    def _():
        for j, array, near in near_pairs:
            near_copy(2 + j, array, near, 2, me - 1).start()

    for k in range(first):

        def send(t, carry, k=k):
            outgoing(k, ways[k][2](t)).start()
            return carry

        lax.fori_loop(0, ways[k][3], send, 0)

    @pl.when(me == 0)
    def _():
        for j, array, near in near_pairs:
            near[0] = jnp.zeros(near.shape[1:], near.dtype)

    @pl.when(me == count - 1)
    def _():
        for j, array, near in near_pairs:
            near[2] = jnp.zeros(near.shape[1:], near.dtype)

    for copy in own:
        copy.wait()

    @pl.when(me > 0)
    def _():
        for j, array, near in near_pairs:
            near_copy(j, array, near, 0, me - 1).wait_recv()

    @pl.when(me < count - 1)
    def _():
        for j, array, near in near_pairs:
            near_copy(2 + j, array, near, 2, me + 1).wait_recv()

    spans = windows.shape[1]
    tile = (me * rows + lax.broadcasted_iota(jnp.int32, (rows, spans), 0)) // TILE_LEN
    bounds = windows[...]
    inside = (bounds[0:1, :] <= tile) & (tile < bounds[1:2, :])
    inside = jnp.where(inside, 1.0, 0.0).astype(jnp.bfloat16)
    seen = []
    for slot in range(3):
        stretch = lax.broadcasted_iota(jnp.int32, (spans, audio_rows), 1) // STRETCH_LEN
        stretch = stretch + (me + slot - 1) * (audio_rows // STRETCH_LEN)
        picks = stretch == lax.broadcasted_iota(jnp.int32, (spans, audio_rows), 0)
        picks = jnp.where(picks, 1.0, 0.0).astype(jnp.bfloat16)
        part = jnp.dot(inside, picks, preferred_element_type=jnp.float32)
        seen.append(jnp.concatenate([part] * (LANES // AUDIO_DIM), axis=0))

    for b in range(cross_q.shape[1] // LANES):
        lanes = slice(b * LANES, (b + 1) * LANES)
        stacked = lane_heads(local_cq[:, lanes])
        scores = []
        for slot in range(3):
            part = lax.dot_general(
                stacked,
                near_k[slot, :, lanes],
                (((1,), (1,)), ((), ())),
                preferred_element_type=jnp.float32,
            )
            scores.append(jnp.where(seen[slot] > 0.5, part, jnp.float32(-1e30)))
        peak = jnp.max(jnp.maximum(jnp.maximum(scores[0], scores[1]), scores[2]), axis=1, keepdims=True)
        factor = jnp.float32(audio_scaling * math.log2(math.e))
        weights = [jnp.exp2((part - peak) * factor) for part in scores]
        summed = jnp.sum(weights[0] + weights[1] + weights[2], axis=1, keepdims=True)
        mixed = sum(
            jnp.dot(
                weights[slot].astype(jnp.bfloat16),
                near_v[slot, :, lanes],
                preferred_element_type=jnp.float32,
            )
            for slot in range(3)
        )
        video_cross[:, lanes] = merge_lane_heads(mixed / summed, rows).astype(jnp.bfloat16)

    def await_stream(k):
        kept(k).wait()

        def one(t, carry):
            incoming(k, ways[k][2](t)).wait_recv()
            return carry

        lax.fori_loop(0, ways[k][3], one, 0)

    def run_blocks(k, steps, mix):
        def one(t, carry):
            mix(ways[k][2](t))

            @pl.when(t > 0)
            def _():
                outgoing(k, ways[k][2](t - 1)).start()

            return carry

        lax.fori_loop(0, steps, one, 0)
        kept(k).start()

    def part_copy(j, array, land):
        return pltpu.make_async_remote_copy(
            src_ref=array,
            dst_ref=land,
            send_sem=part_send.at[j],
            recv_sem=part_recv.at[j],
            device_id=device((me + half) % count),
            device_id_type=pl.DeviceIdType.MESH,
        )

    part_copies = [part_copy(0, far_part, got_part), part_copy(1, far_stat, got_stat)]
    stat_lane = lax.broadcasted_iota(jnp.int32, (audio_rows, LANES), 1)
    each = LANES // AUDIO_DIM

    def audio_parts(first_source, part, stat):
        def one(j, stats):
            queries = land_aq[first_source + j]
            for b in range(blocks_each):
                lanes = slice(b * LANES, (b + 1) * LANES)
                mixed, peak, summed = softmax_mix(
                    lane_heads(queries[:, lanes]), land_ck[:, lanes], land_cv[:, lanes], audio_scaling
                )
                part[j, :, lanes] = merge_lane_heads(mixed, audio_rows).astype(part.dtype)
                level = peak * jnp.float32(audio_scaling * math.log2(math.e)) + jnp.log2(summed)
                for i in range(each):
                    stats = jnp.where(
                        stat_lane == (j * blocks_each + b) * each + i,
                        level[i * audio_rows : (i + 1) * audio_rows],
                        stats,
                    )
            return stats

        stat[...] = lax.fori_loop(0, half, one, jnp.zeros((audio_rows, LANES), jnp.float32))

    def merge_parts(peer):
        j = peer % half
        for b in range(blocks_each):
            lanes = slice(b * LANES, (b + 1) * LANES)
            shares = []
            for i in range(each):
                picked = stat_lane == (j * blocks_each + b) * each + i
                mine = jnp.sum(jnp.where(picked, own_stat[...], 0.0), axis=1, keepdims=True)
                other = jnp.sum(jnp.where(picked, got_stat[...], 0.0), axis=1, keepdims=True)
                peak = jnp.maximum(mine, other)
                mine = jnp.exp2(mine - peak)
                other = jnp.exp2(other - peak)
                total = mine + other
                shares.append((mine / total, other / total))
            own_share, got_share = (
                merge_lane_heads(
                    jnp.concatenate(
                        [jnp.broadcast_to(s[w], (audio_rows, LANES)) for s in shares], axis=0
                    ),
                    audio_rows,
                )
                for w in range(2)
            )
            merged = own_part[j, :, lanes] * own_share
            merged = merged + got_part[j, :, lanes].astype(jnp.float32) * got_share
            mixed_a[j, :, lanes] = merged.astype(jnp.bfloat16)

    for h in range(video_each):
        for k in video_ways[h]:
            await_stream(k)

        def mix_video(source, h=h):
            mixed, peak, summed = softmax_mix(
                land_q[h, row(source), :], land_k[h], land_v[h], video_scaling
            )
            mixed_v[h, row(source), :] = mixed.astype(jnp.bfloat16)

        run_blocks(first + h, count, mix_video)
        if h == 0:
            for k in audio_ways:
                await_stream(k)
            audio_parts((1 - side) * half, far_part, far_stat)
            audio_parts(side * half, own_part, own_stat)
            for copy in part_copies:
                copy.start()
    for copy in part_copies:
        copy.wait()
    run_blocks(len(ways) - 1, half, merge_parts)

    for k in range(len(ways)):

        def sent(t, carry, k=k):
            outgoing(k, ways[k][2](t)).wait_send()
            return carry

        lax.fori_loop(0, ways[k][3], sent, 0)
    for k in range(first, len(ways)):
        await_stream(k)

    @pl.when(me < count - 1)
    def _():
        for j, array, near in near_pairs:
            near_copy(j, array, near, 0, me + 1).wait_send()

    @pl.when(me > 0)
    def _():
        for j, array, near in near_pairs:
            near_copy(2 + j, array, near, 2, me - 1).wait_send()


def store_kernel(*refs):
    copies = [pltpu.make_async_copy(refs[i], refs[3 + i], refs[6].at[i]) for i in range(3)]
    for copy in copies:
        copy.start()
    for copy in copies:
        copy.wait()


def exchanged_body(count, sub_count, *arrays):
    vid_q, vid_k, vid_v, aud_q, cross_k, cross_v, cross_q, aud_k, aud_v, windows = arrays
    rows = vid_q.shape[0]
    audio_rows = aud_q.shape[0]
    video_each = vid_q.shape[1] // HEAD_DIM // count
    halves = count // 2
    width = aud_q.shape[1] // halves
    kinds = 4 * video_each + 4
    half = jnp.bfloat16
    place = pl.BlockSpec(memory_space=pl.ANY)
    held = pl.pallas_call(
        partial(exchange_kernel, count, sub_count),
        out_shape=tuple(pltpu.VMEM(a.shape, half) for a in (vid_q, aud_q, cross_q)),
        in_specs=[place] * 9 + [pl.BlockSpec(memory_space=pltpu.VMEM)],
        out_specs=(pl.BlockSpec(memory_space=pltpu.VMEM),) * 3,
        scratch_shapes=[
            pltpu.VMEM((video_each, count * rows, HEAD_DIM), half),
            pltpu.VMEM((video_each, count * rows, HEAD_DIM), half),
            pltpu.VMEM((video_each, count * rows, HEAD_DIM), half),
            pltpu.VMEM((count, audio_rows, width), half),
            pltpu.VMEM((halves * rows, width), half),
            pltpu.VMEM((halves * rows, width), half),
            pltpu.VMEM((video_each, count * rows, HEAD_DIM), half),
            pltpu.VMEM((halves, audio_rows, width), half),
            pltpu.VMEM((halves, audio_rows, width), jnp.float32),
            pltpu.VMEM((audio_rows, LANES), jnp.float32),
            pltpu.VMEM((halves, audio_rows, width), half),
            pltpu.VMEM((audio_rows, LANES), jnp.float32),
            pltpu.VMEM((halves, audio_rows, width), half),
            pltpu.VMEM((audio_rows, LANES), jnp.float32),
            pltpu.VMEM((3, audio_rows, aud_k.shape[1]), half),
            pltpu.VMEM((3, audio_rows, aud_k.shape[1]), half),
            pltpu.VMEM(cross_q.shape, half),
            pltpu.SemaphoreType.DMA((kinds, count)),
            pltpu.SemaphoreType.DMA((kinds, count)),
            pltpu.SemaphoreType.DMA((4,)),
            pltpu.SemaphoreType.DMA((4,)),
            pltpu.SemaphoreType.DMA((2,)),
            pltpu.SemaphoreType.DMA((2,)),
            pltpu.SemaphoreType.DMA((3,)),
        ],
        compiler_params=pltpu.CompilerParams(collective_id=0, has_side_effects=True),
        name="joint_attention",
    )(*arrays)
    return pl.pallas_call(
        store_kernel,
        out_shape=tuple(jax.ShapeDtypeStruct(a.shape, half) for a in (vid_q, aud_q, cross_q)),
        in_specs=[pl.BlockSpec(memory_space=pltpu.VMEM)] * 3,
        out_specs=(place, place, place),
        scratch_shapes=[pltpu.SemaphoreType.DMA((3,))],
        name="store_results",
    )(*[pltpu.with_memory_space_constraint(x, pltpu.VMEM) for x in held])


def body(*arrays):
    sub_count = lax.axis_size("sub")
    count = lax.axis_size("seq") * sub_count
    video_heads = arrays[0].shape[1] // HEAD_DIM
    audio_heads = arrays[3].shape[1] // AUDIO_DIM
    halved = lax.axis_size("seq") % 2 == 0 and audio_heads <= LANES
    if halved and video_heads % count == 0 and audio_heads % count == 0:
        return exchanged_body(count, sub_count, *arrays)
    return gathered_body(*arrays)


def solution(mesh):
    return jax.shard_map(
        body,
        mesh=mesh,
        in_specs=(
            P(("grp", "seq", "sub"), "head"),
            P(("grp", "seq", "sub"), "head"),
            P(("grp", "seq", "sub"), "head"),
            P(("grp", "seq", "sub"), "head"),
            P(("grp", "seq", "sub"), "head"),
            P(("grp", "seq", "sub"), "head"),
            P(("grp", "seq", "sub"), "head"),
            P(("grp", "seq", "sub"), "head"),
            P(("grp", "seq", "sub"), "head"),
            P(None, "grp"),
        ),
        out_specs=(
            P(("grp", "seq", "sub"), "head"),
            P(("grp", "seq", "sub"), "head"),
            P(("grp", "seq", "sub"), "head"),
        ),
        check_vma=False,
    )
```

```python
from functools import partial
import math

import jax
import jax.numpy as jnp
from jax import lax
from jax.experimental import pallas as pl
from jax.experimental.pallas import tpu as pltpu
from jax.sharding import PartitionSpec as P

HEAD_DIM = 128
AUDIO_DIM = 64
TILE_LEN = 32
STRETCH_LEN = 8


def extended(cells, sides, width):
    for axis, dim in sides:
        count = lax.axis_size(axis)
        ends = count - 1
        head = lax.slice_in_dim(cells, 0, width, axis=dim)
        tail = lax.slice_in_dim(cells, cells.shape[dim] - width, cells.shape[dim], axis=dim)
        cells = jnp.concatenate(
            [
                lax.ppermute(tail, axis, [(i, (i + 1) % count) for i in range(ends)]),
                cells,
                lax.ppermute(head, axis, [((i + 1) % count, i) for i in range(ends)]),
            ],
            axis=dim,
        )
    return cells


def start_state(query_count, head_count, head_size):
    running = jnp.full((head_count, query_count), -jnp.inf, jnp.float32)
    summed = jnp.zeros((head_count, query_count), jnp.float32)
    numerator = jnp.zeros((head_count, query_count, head_size), jnp.float32)
    return (running, summed, numerator)


def absorb(state_in, queries, key_rows, value_rows, head_count, scaling, visible):
    running, summed, numerator = state_in
    query_count = queries.shape[0]
    key_count = key_rows.shape[0]
    head_size = queries.shape[1] // head_count
    scores = (
        jnp.einsum(
            "qhe,khe->hqk",
            queries.reshape(query_count, head_count, head_size),
            key_rows.reshape(key_count, head_count, head_size),
            preferred_element_type=jnp.float32,
        )
        * scaling
    )
    if visible is not None:
        scores = jnp.where(visible[None], scores, jnp.float32(-1e30))
    newest = jnp.maximum(running, jnp.max(scores, axis=2))
    shrink = jnp.exp(running - newest)
    weights = jnp.exp(scores - newest[:, :, None])
    summed = summed * shrink + jnp.sum(weights, axis=2)
    numerator = numerator * shrink[:, :, None] + jnp.einsum(
        "hqk,khe->hqe",
        weights.astype(jnp.bfloat16),
        value_rows.reshape(key_count, head_count, head_size),
        preferred_element_type=jnp.float32,
    )
    return (newest, summed, numerator)


def block_split(total_rows):
    block_rows = total_rows
    while block_rows > 512 and block_rows % 2 == 0:
        block_rows = block_rows // 2
    return (block_rows, total_rows // block_rows)


def fold_keys(state_in, shards_in, offset, queries, head_count, scaling):
    key_rows, value_rows = shards_in
    block_rows, block_count = block_split(key_rows.shape[0])
    key_blocks = key_rows.reshape(block_count, block_rows, key_rows.shape[1])
    value_blocks = value_rows.reshape(block_count, block_rows, value_rows.shape[1])

    def one_block(state, paired):
        return (absorb(state, queries, paired[0], paired[1], head_count, scaling, None), None)

    result, unused = lax.scan(one_block, state_in, (key_blocks, value_blocks))
    return result


def normalize_heads(state_in):
    running, summed, numerator = state_in
    mixed = numerator / summed[:, :, None]
    return mixed.transpose(1, 0, 2).reshape(mixed.shape[1], -1).astype(jnp.bfloat16)


def gathered_body(vid_q, vid_k, vid_v, aud_q, cross_k, cross_v, cross_q, aud_k, aud_v, windows):
    video_heads = vid_q.shape[1] // HEAD_DIM
    video_scaling = 1.0 / math.sqrt(HEAD_DIM)
    audio_heads = aud_q.shape[1] // AUDIO_DIM
    audio_scaling = 1.0 / math.sqrt(AUDIO_DIM)
    moved_q, moved_k, moved_v = (
        lax.all_to_all(vid_q, "sub", split_axis=1, concat_axis=0, tiled=True),
        lax.all_to_all(vid_k, "sub", split_axis=1, concat_axis=0, tiled=True),
        lax.all_to_all(vid_v, "sub", split_axis=1, concat_axis=0, tiled=True),
    )
    pair_heads = video_heads // lax.axis_size("sub")
    folder = partial(fold_keys, queries=moved_q, head_count=pair_heads, scaling=video_scaling)
    state = folder(
        start_state(moved_q.shape[0], pair_heads, HEAD_DIM),
        (
            lax.all_gather(moved_k, "seq", axis=0, tiled=True),
            lax.all_gather(moved_v, "seq", axis=0, tiled=True),
        ),
        jnp.int32(0),
    )
    video_self = lax.all_to_all(
        normalize_heads(state), "sub", split_axis=0, concat_axis=1, tiled=True
    )
    folder = partial(fold_keys, queries=aud_q, head_count=audio_heads, scaling=audio_scaling)
    state = folder(
        start_state(aud_q.shape[0], audio_heads, AUDIO_DIM),
        (
            lax.all_gather(cross_k, ("seq", "sub"), axis=0, tiled=True),
            lax.all_gather(cross_v, ("seq", "sub"), axis=0, tiled=True),
        ),
        jnp.int32(0),
    )
    audio_out = normalize_heads(state)
    audio_rows = aud_k.shape[0]
    key_width = aud_k.shape[1]
    padded_rows = extended(
        jnp.concatenate((aud_k, aud_v), axis=1), ((("seq", "sub"), 0),), audio_rows
    )
    near_keys = padded_rows[:, :key_width]
    near_values = padded_rows[:, key_width:]
    position = lax.axis_index(("seq", "sub"))
    audio_index = (position - 1) * audio_rows + jnp.arange(padded_rows.shape[0], dtype=jnp.int32)
    stretch_index = audio_index // STRETCH_LEN
    stretch_ids = jnp.arange(windows.shape[1], dtype=jnp.int32)
    onehot = stretch_index[:, None] == stretch_ids[None, :]
    first_tile = jnp.sum(jnp.where(onehot, windows[0][None, :], 0), axis=1)
    after_tile = jnp.sum(jnp.where(onehot, windows[1][None, :], 0), axis=1)
    video_rows = cross_q.shape[0]
    video_tile = (position * video_rows + jnp.arange(video_rows, dtype=jnp.int32)) // TILE_LEN
    visible = (first_tile[None, :] <= video_tile[:, None]) & (
        video_tile[:, None] < after_tile[None, :]
    )
    state = absorb(
        start_state(video_rows, audio_heads, AUDIO_DIM),
        cross_q,
        near_keys,
        near_values,
        audio_heads,
        audio_scaling,
        visible,
    )
    video_cross = normalize_heads(state)
    return (video_self, audio_out, video_cross)


LANES = 128
AXES = ("seq", "sub")


def softmax_mix(queries, key_rows, value_rows, scaling):
    scores = lax.dot_general(
        queries, key_rows, (((1,), (1,)), ((), ())), preferred_element_type=jnp.float32
    )
    peak = jnp.max(scores, axis=1, keepdims=True)
    weights = jnp.exp2((scores - peak) * jnp.float32(scaling * math.log2(math.e)))
    summed = jnp.sum(weights, axis=1, keepdims=True)
    mixed = jnp.dot(
        weights.astype(jnp.bfloat16), value_rows, preferred_element_type=jnp.float32
    )
    return mixed / summed, peak, summed


def lane_heads(block):
    wide = block.astype(jnp.float32)
    lane = lax.broadcasted_iota(jnp.int32, wide.shape, 1) // AUDIO_DIM
    parts = [jnp.where(lane == i, wide, 0.0) for i in range(LANES // AUDIO_DIM)]
    return jnp.concatenate(parts, axis=0).astype(jnp.bfloat16)


def merge_lane_heads(stacked, rows):
    lane = lax.broadcasted_iota(jnp.int32, (rows, LANES), 1) // AUDIO_DIM
    merged = stacked[:rows]
    for i in range(1, LANES // AUDIO_DIM):
        merged = jnp.where(lane == i, stacked[i * rows : (i + 1) * rows], merged)
    return merged


def exchange_kernel(
    count,
    sub_count,
    vid_q,
    vid_k,
    vid_v,
    aud_q,
    cross_k,
    cross_v,
    cross_q,
    aud_k,
    aud_v,
    windows,
    video_self,
    audio_out,
    video_cross,
    land_q,
    land_k,
    land_v,
    land_aq,
    land_ck,
    land_cv,
    mixed_v,
    mixed_a,
    own_part,
    own_stat,
    far_part,
    far_stat,
    got_part,
    got_stat,
    near_k,
    near_v,
    local_cq,
    send_sem,
    recv_sem,
    near_send,
    near_recv,
    part_send,
    part_recv,
    local_sem,
):
    rows = vid_q.shape[0]
    audio_rows = aud_q.shape[0]
    video_each = vid_q.shape[1] // HEAD_DIM // count
    half = count // 2
    blocks_each = aud_q.shape[1] // LANES // half
    width = blocks_each * LANES
    video_scaling = 1.0 / math.sqrt(HEAD_DIM)
    audio_scaling = 1.0 / math.sqrt(AUDIO_DIM)
    me = lax.axis_index("seq") * sub_count + lax.axis_index("sub")

    side = me // half
    place = me % half

    def device(peer):
        return {"seq": peer // sub_count, "sub": peer % sub_count}

    def peer_at(t):
        return ((side + 1 - t // half) % 2) * half + (place + t + t // half) % half

    def peer_near(t):
        return side * half + (place + 1 + t) % half

    barrier = pltpu.get_barrier_semaphore()

    def greet(t, carry):
        pl.semaphore_signal(
            barrier, inc=1, device_id=device(peer_at(t)), device_id_type=pl.DeviceIdType.MESH
        )
        return carry

    lax.fori_loop(0, count - 1, greet, 0)

    own = [
        pltpu.make_async_copy(cross_q, local_cq, local_sem.at[0]),
        pltpu.make_async_copy(aud_k, near_k.at[1], local_sem.at[1]),
        pltpu.make_async_copy(aud_v, near_v.at[1], local_sem.at[2]),
    ]
    for copy in own:
        copy.start()

    def column(index):
        return pl.ds(pl.multiple_of(index * LANES, LANES), LANES)

    def row(index):
        return pl.ds(pl.multiple_of(index * rows, rows), rows)

    def columns(index):
        return pl.ds(pl.multiple_of(index * width, LANES), width)

    def video_way(array, land, h):
        return (
            lambda peer: array.at[:, column(peer * video_each + h)],
            lambda source: land.at[h, row(source), :],
            peer_at,
            count - 1,
        )

    def half_way(array, land):
        return (
            lambda peer: array.at[:, columns(peer % half)],
            lambda source: land.at[row(source % half), :],
            peer_near,
            half - 1,
        )

    ways = [
        (
            lambda peer: aud_q.at[:, columns(peer % half)],
            lambda source: land_aq.at[source],
            peer_at,
            count - 1,
        )
    ]
    audio_ways = [0]
    video_ways = []
    for h in range(video_each):
        video_ways.append(list(range(len(ways), len(ways) + 3)))
        for array, land in ((vid_k, land_k), (vid_v, land_v), (vid_q, land_q)):
            ways.append(video_way(array, land, h))
        if h == 0:
            for array, land in ((cross_k, land_ck), (cross_v, land_cv)):
                audio_ways.append(len(ways))
                ways.append(half_way(array, land))
    first = len(ways)
    for h in range(video_each):
        ways.append(
            (
                lambda peer, h=h: mixed_v.at[h, row(peer), :],
                lambda source, h=h: video_self.at[:, column(source * video_each + h)],
                peer_at,
                count - 1,
            )
        )
    ways.append(
        (
            lambda peer: mixed_a.at[peer % half],
            lambda source: audio_out.at[:, columns(source % half)],
            peer_near,
            half - 1,
        )
    )

    def outgoing(k, peer):
        return pltpu.make_async_remote_copy(
            src_ref=ways[k][0](peer),
            dst_ref=ways[k][1](me),
            send_sem=send_sem.at[k, peer],
            recv_sem=recv_sem.at[k, me],
            device_id=device(peer),
            device_id_type=pl.DeviceIdType.MESH,
        )

    def incoming(k, peer):
        return pltpu.make_async_remote_copy(
            src_ref=ways[k][0](peer),
            dst_ref=ways[k][1](peer),
            send_sem=send_sem.at[k, peer],
            recv_sem=recv_sem.at[k, peer],
            device_id=device(peer),
            device_id_type=pl.DeviceIdType.MESH,
        )

    def kept(k):
        return pltpu.make_async_copy(ways[k][0](me), ways[k][1](me), send_sem.at[k, me])

    def near_copy(j, array, near, side, peer):
        return pltpu.make_async_remote_copy(
            src_ref=array,
            dst_ref=near.at[side],
            send_sem=near_send.at[j],
            recv_sem=near_recv.at[j],
            device_id=device(peer),
            device_id_type=pl.DeviceIdType.MESH,
        )

    for k in range(first):
        kept(k).start()
    pl.semaphore_wait(barrier, count - 1)

    near_pairs = ((0, aud_k, near_k), (1, aud_v, near_v))

    @pl.when(me < count - 1)
    def _():
        for j, array, near in near_pairs:
            near_copy(j, array, near, 0, me + 1).start()

    @pl.when(me > 0)
    def _():
        for j, array, near in near_pairs:
            near_copy(2 + j, array, near, 2, me - 1).start()

    for k in range(first):

        def send(t, carry, k=k):
            outgoing(k, ways[k][2](t)).start()
            return carry

        lax.fori_loop(0, ways[k][3], send, 0)

    @pl.when(me == 0)
    def _():
        for j, array, near in near_pairs:
            near[0] = jnp.zeros(near.shape[1:], near.dtype)

    @pl.when(me == count - 1)
    def _():
        for j, array, near in near_pairs:
            near[2] = jnp.zeros(near.shape[1:], near.dtype)

    for copy in own:
        copy.wait()

    @pl.when(me > 0)
    def _():
        for j, array, near in near_pairs:
            near_copy(j, array, near, 0, me - 1).wait_recv()

    @pl.when(me < count - 1)
    def _():
        for j, array, near in near_pairs:
            near_copy(2 + j, array, near, 2, me + 1).wait_recv()

    spans = windows.shape[1]
    tile = (me * rows + lax.broadcasted_iota(jnp.int32, (rows, spans), 0)) // TILE_LEN
    bounds = windows[...]
    inside = (bounds[0:1, :] <= tile) & (tile < bounds[1:2, :])
    inside = jnp.where(inside, 1.0, 0.0).astype(jnp.bfloat16)
    seen = []
    for slot in range(3):
        stretch = lax.broadcasted_iota(jnp.int32, (spans, audio_rows), 1) // STRETCH_LEN
        stretch = stretch + (me + slot - 1) * (audio_rows // STRETCH_LEN)
        picks = stretch == lax.broadcasted_iota(jnp.int32, (spans, audio_rows), 0)
        picks = jnp.where(picks, 1.0, 0.0).astype(jnp.bfloat16)
        part = jnp.dot(inside, picks, preferred_element_type=jnp.float32)
        seen.append(jnp.concatenate([part] * (LANES // AUDIO_DIM), axis=0))

    for b in range(cross_q.shape[1] // LANES):
        lanes = slice(b * LANES, (b + 1) * LANES)
        stacked = lane_heads(local_cq[:, lanes])
        scores = []
        for slot in range(3):
            part = lax.dot_general(
                stacked,
                near_k[slot, :, lanes],
                (((1,), (1,)), ((), ())),
                preferred_element_type=jnp.float32,
            )
            scores.append(jnp.where(seen[slot] > 0.5, part, jnp.float32(-1e30)))
        peak = jnp.max(jnp.maximum(jnp.maximum(scores[0], scores[1]), scores[2]), axis=1, keepdims=True)
        factor = jnp.float32(audio_scaling * math.log2(math.e))
        weights = [jnp.exp2((part - peak) * factor) for part in scores]
        summed = jnp.sum(weights[0] + weights[1] + weights[2], axis=1, keepdims=True)
        mixed = sum(
            jnp.dot(
                weights[slot].astype(jnp.bfloat16),
                near_v[slot, :, lanes],
                preferred_element_type=jnp.float32,
            )
            for slot in range(3)
        )
        video_cross[:, lanes] = merge_lane_heads(mixed / summed, rows).astype(jnp.bfloat16)

    def await_stream(k):
        kept(k).wait()

        def one(t, carry):
            incoming(k, ways[k][2](t)).wait_recv()
            return carry

        lax.fori_loop(0, ways[k][3], one, 0)

    def run_blocks(k, steps, mix):
        def one(t, carry):
            mix(ways[k][2](t))

            @pl.when(t > 0)
            def _():
                outgoing(k, ways[k][2](t - 1)).start()

            return carry

        lax.fori_loop(0, steps, one, 0)
        kept(k).start()

    def part_copy(j, array, land):
        return pltpu.make_async_remote_copy(
            src_ref=array,
            dst_ref=land,
            send_sem=part_send.at[j],
            recv_sem=part_recv.at[j],
            device_id=device((me + half) % count),
            device_id_type=pl.DeviceIdType.MESH,
        )

    part_copies = [part_copy(0, far_part, got_part), part_copy(1, far_stat, got_stat)]
    stat_lane = lax.broadcasted_iota(jnp.int32, (audio_rows, LANES), 1)
    each = LANES // AUDIO_DIM

    def audio_parts(first_source, part, stat):
        def one(j, stats):
            queries = land_aq[first_source + j]
            for b in range(blocks_each):
                lanes = slice(b * LANES, (b + 1) * LANES)
                mixed, peak, summed = softmax_mix(
                    lane_heads(queries[:, lanes]), land_ck[:, lanes], land_cv[:, lanes], audio_scaling
                )
                part[j, :, lanes] = merge_lane_heads(mixed, audio_rows).astype(part.dtype)
                level = peak * jnp.float32(audio_scaling * math.log2(math.e)) + jnp.log2(summed)
                for i in range(each):
                    stats = jnp.where(
                        stat_lane == (j * blocks_each + b) * each + i,
                        level[i * audio_rows : (i + 1) * audio_rows],
                        stats,
                    )
            return stats

        stats = lax.fori_loop(0, half, one, jnp.zeros((audio_rows, LANES), jnp.float32))
        padded = jnp.concatenate(
            [stats, jnp.zeros((LANES - audio_rows, LANES), jnp.float32)], axis=0
        )
        stat[...] = padded.T[: stat.shape[0]]

    def merge_parts(peer):
        j = peer % half
        unpacked = []
        for stat in (own_stat, got_stat):
            rest = jnp.zeros((LANES - stat.shape[0], LANES), jnp.float32)
            unpacked.append(jnp.concatenate([stat[...], rest], axis=0).T[:audio_rows])
        for b in range(blocks_each):
            lanes = slice(b * LANES, (b + 1) * LANES)
            shares = []
            for i in range(each):
                picked = stat_lane == (j * blocks_each + b) * each + i
                mine = jnp.sum(jnp.where(picked, unpacked[0], 0.0), axis=1, keepdims=True)
                other = jnp.sum(jnp.where(picked, unpacked[1], 0.0), axis=1, keepdims=True)
                peak = jnp.maximum(mine, other)
                mine = jnp.exp2(mine - peak)
                other = jnp.exp2(other - peak)
                total = mine + other
                shares.append((mine / total, other / total))
            own_share, got_share = (
                merge_lane_heads(
                    jnp.concatenate(
                        [jnp.broadcast_to(s[w], (audio_rows, LANES)) for s in shares], axis=0
                    ),
                    audio_rows,
                )
                for w in range(2)
            )
            merged = own_part[j, :, lanes] * own_share
            merged = merged + got_part[j, :, lanes].astype(jnp.float32) * got_share
            mixed_a[j, :, lanes] = merged.astype(jnp.bfloat16)

    for h in range(video_each):
        for k in video_ways[h]:
            await_stream(k)

        def mix_video(source, h=h):
            mixed, peak, summed = softmax_mix(
                land_q[h, row(source), :], land_k[h], land_v[h], video_scaling
            )
            mixed_v[h, row(source), :] = mixed.astype(jnp.bfloat16)

        run_blocks(first + h, count, mix_video)
        if h == 0:
            for k in audio_ways:
                await_stream(k)
            audio_parts((1 - side) * half, far_part, far_stat)
            audio_parts(side * half, own_part, own_stat)
            for copy in part_copies:
                copy.start()
    for copy in part_copies:
        copy.wait()
    run_blocks(len(ways) - 1, half, merge_parts)

    for k in range(len(ways)):

        def sent(t, carry, k=k):
            outgoing(k, ways[k][2](t)).wait_send()
            return carry

        lax.fori_loop(0, ways[k][3], sent, 0)
    for k in range(first, len(ways)):
        await_stream(k)

    @pl.when(me < count - 1)
    def _():
        for j, array, near in near_pairs:
            near_copy(j, array, near, 0, me + 1).wait_send()

    @pl.when(me > 0)
    def _():
        for j, array, near in near_pairs:
            near_copy(2 + j, array, near, 2, me - 1).wait_send()


def store_kernel(*refs):
    copies = [pltpu.make_async_copy(refs[i], refs[3 + i], refs[6].at[i]) for i in range(3)]
    for copy in copies:
        copy.start()
    for copy in copies:
        copy.wait()


def exchanged_body(count, sub_count, *arrays):
    vid_q, vid_k, vid_v, aud_q, cross_k, cross_v, cross_q, aud_k, aud_v, windows = arrays
    rows = vid_q.shape[0]
    audio_rows = aud_q.shape[0]
    video_each = vid_q.shape[1] // HEAD_DIM // count
    halves = count // 2
    width = aud_q.shape[1] // halves
    kinds = 4 * video_each + 4
    levels = -(-aud_q.shape[1] // AUDIO_DIM // 8) * 8
    half = jnp.bfloat16
    place = pl.BlockSpec(memory_space=pl.ANY)
    held = pl.pallas_call(
        partial(exchange_kernel, count, sub_count),
        out_shape=tuple(pltpu.VMEM(a.shape, half) for a in (vid_q, aud_q, cross_q)),
        in_specs=[place] * 9 + [pl.BlockSpec(memory_space=pltpu.VMEM)],
        out_specs=(pl.BlockSpec(memory_space=pltpu.VMEM),) * 3,
        scratch_shapes=[
            pltpu.VMEM((video_each, count * rows, HEAD_DIM), half),
            pltpu.VMEM((video_each, count * rows, HEAD_DIM), half),
            pltpu.VMEM((video_each, count * rows, HEAD_DIM), half),
            pltpu.VMEM((count, audio_rows, width), half),
            pltpu.VMEM((halves * rows, width), half),
            pltpu.VMEM((halves * rows, width), half),
            pltpu.VMEM((video_each, count * rows, HEAD_DIM), half),
            pltpu.VMEM((halves, audio_rows, width), half),
            pltpu.VMEM((halves, audio_rows, width), jnp.float32),
            pltpu.VMEM((levels, LANES), jnp.float32),
            pltpu.VMEM((halves, audio_rows, width), half),
            pltpu.VMEM((levels, LANES), jnp.float32),
            pltpu.VMEM((halves, audio_rows, width), half),
            pltpu.VMEM((levels, LANES), jnp.float32),
            pltpu.VMEM((3, audio_rows, aud_k.shape[1]), half),
            pltpu.VMEM((3, audio_rows, aud_k.shape[1]), half),
            pltpu.VMEM(cross_q.shape, half),
            pltpu.SemaphoreType.DMA((kinds, count)),
            pltpu.SemaphoreType.DMA((kinds, count)),
            pltpu.SemaphoreType.DMA((4,)),
            pltpu.SemaphoreType.DMA((4,)),
            pltpu.SemaphoreType.DMA((2,)),
            pltpu.SemaphoreType.DMA((2,)),
            pltpu.SemaphoreType.DMA((3,)),
        ],
        compiler_params=pltpu.CompilerParams(collective_id=0, has_side_effects=True),
        name="joint_attention",
    )(*arrays)
    return pl.pallas_call(
        store_kernel,
        out_shape=tuple(jax.ShapeDtypeStruct(a.shape, half) for a in (vid_q, aud_q, cross_q)),
        in_specs=[pl.BlockSpec(memory_space=pltpu.VMEM)] * 3,
        out_specs=(place, place, place),
        scratch_shapes=[pltpu.SemaphoreType.DMA((3,))],
        name="store_results",
    )(*[pltpu.with_memory_space_constraint(x, pltpu.VMEM) for x in held])


def body(*arrays):
    sub_count = lax.axis_size("sub")
    count = lax.axis_size("seq") * sub_count
    video_heads = arrays[0].shape[1] // HEAD_DIM
    audio_heads = arrays[3].shape[1] // AUDIO_DIM
    halved = lax.axis_size("seq") % 2 == 0 and max(audio_heads, arrays[3].shape[0]) <= LANES
    if halved and video_heads % count == 0 and audio_heads % count == 0:
        return exchanged_body(count, sub_count, *arrays)
    return gathered_body(*arrays)


def solution(mesh):
    return jax.shard_map(
        body,
        mesh=mesh,
        in_specs=(
            P(("grp", "seq", "sub"), "head"),
            P(("grp", "seq", "sub"), "head"),
            P(("grp", "seq", "sub"), "head"),
            P(("grp", "seq", "sub"), "head"),
            P(("grp", "seq", "sub"), "head"),
            P(("grp", "seq", "sub"), "head"),
            P(("grp", "seq", "sub"), "head"),
            P(("grp", "seq", "sub"), "head"),
            P(("grp", "seq", "sub"), "head"),
            P(None, "grp"),
        ),
        out_specs=(
            P(("grp", "seq", "sub"), "head"),
            P(("grp", "seq", "sub"), "head"),
            P(("grp", "seq", "sub"), "head"),
        ),
        check_vma=False,
    )
```
